256 devices in a mesh: band: 16 (over y, x_lo, core), grid: 16 (over z, x_hi).
Axes of the slice: x: 4 (x_hi: 2, x_lo: 2; x = x_hi * 2 + x_lo), y: 4, z: 8, core: 2. Of those that a mesh axis runs over, the one named last changes fastest.
Arguments:
- own_orbitals: bfloat16 [32, 128, 128, 128], P('band', 'grid'), may hold values from -9 to 9
- resident_orbitals: bfloat16 [32, 128, 128, 128], P('band', 'grid'), may hold values from -9 to 9
- pair_lists: int32 [16, 2, 2, 2], P('band'), may hold values from 0 to 1, as said below
- pair_counts: int32 [16, 2], P('band'), may hold values from 1 to 2, as said below
Outputs:
- exchange_block: bfloat16 [32, 128, 128, 128], P('band', 'grid')
- intersection: float32 [32, 2], P('band')
The draws below stay inside these ranges and needn't reach their ends.
Inputs may be any that keep to these rules, and one draw needn't show every extreme that they name: pair_lists[b, l, s] = (i, j) pairs band i of block b with band j of the partner block of list l; the 2 pairs of one list are distinct; slots s >= pair_counts[b, l] hold pairs that are not used. `pair_counts`: in each of the two lists exactly one block has 2 live slots, every other block exactly 1.
All inputs are finite; a program needn't handle non-finite values.
Results may differ from the reference program's by a relative error of at most 0.00045.
Values may be sent and summed in bfloat16 or wider, within the bound.
No kernel may reach another device: no remote copies, remote signals or barrier semaphores. Data moves between devices by JAX's collectives and lax.ppermute only.
A program may use at most 64 MiB of HBM per device.

```python
import jax
import jax.numpy as jnp
from jax import lax

NG = 128
BANDS_DEV = 2
PAIRS = 2
BLOCKS = 16
BANDS = 32


def orbital_field(key, salt):
    subkey = jax.random.fold_in(key, salt)
    planes = jnp.arange(NG, dtype=jnp.float32) / NG
    envelope = (0.6 * 3.0 ** planes)[None, :, None, None]
    noise = jnp.clip(jax.random.normal(subkey, (BANDS, NG, NG, NG), jnp.float32), -5.0, 5.0)
    field = envelope * noise
    return field.astype(jnp.bfloat16)


def draw_own_orbitals(key, part):
    return orbital_field(key, 4101)


def draw_resident_orbitals(key, part):
    return orbital_field(key, 4202)


def pair_tables(key):
    base = jax.random.fold_in(key, 7001)
    count_key, hot_key, perm_key = jax.random.split(base, 3)
    light = jax.random.randint(count_key, (BLOCKS, 2), 1, PAIRS, dtype=jnp.int32)
    hottest = jax.random.randint(hot_key, (2,), 0, BLOCKS, dtype=jnp.int32)
    block_ids = jnp.arange(BLOCKS, dtype=jnp.int32)
    counts = jnp.where(block_ids[:, None] == hottest[None, :], PAIRS, light).astype(jnp.int32)
    list_keys = jax.random.split(perm_key, BLOCKS * 2)

    def pick_codes(subkey):
        return jax.random.permutation(subkey, BANDS_DEV * BANDS_DEV)[:PAIRS]
    codes = jax.vmap(pick_codes)(list_keys).reshape(BLOCKS, 2, PAIRS).astype(jnp.int32)
    pairs = jnp.stack([codes // BANDS_DEV, codes % BANDS_DEV], axis=-1).astype(jnp.int32)
    return (pairs, counts)


def draw_pair_lists(key, part):
    return pair_tables(key)[0]


def draw_pair_counts(key, part):
    return pair_tables(key)[1]


def setup_inputs(seed: int = 0) -> dict:
    key_of = jax.random.split(jax.random.key(seed), 5)
    own_orbitals = draw_own_orbitals(jax.random.fold_in(key_of[4], 71), 0)
    resident_orbitals = draw_resident_orbitals(jax.random.fold_in(key_of[4], 71), 0)
    pair_lists = draw_pair_lists(jax.random.fold_in(key_of[4], 71), 0)
    pair_counts = draw_pair_counts(jax.random.fold_in(key_of[4], 71), 0)
    return {"own_orbitals": own_orbitals, "resident_orbitals": resident_orbitals, "pair_lists": pair_lists, "pair_counts": pair_counts}


def fold_freq(indices, length):
    return jnp.minimum(indices, length - indices).astype(jnp.float32)


def coulomb(first_freq, middle_freq, last_freq, length):
    squared = (fold_freq(first_freq, length)[:, None, None] ** 2
               + fold_freq(middle_freq, length)[None, :, None] ** 2
               + fold_freq(last_freq, length)[None, None, :] ** 2)
    return jnp.where(squared > 0.5, 0.25 * length ** 1.5 / jnp.maximum(squared, 1.0), 0.0)


def poisson(density, kernel):
    spectrum = jnp.fft.rfftn(density)
    return jnp.fft.irfftn(spectrum * kernel, s=density.shape).astype(jnp.float32)


def reference(own_orbitals, resident_orbitals, pair_lists, pair_counts):
    received = jnp.roll(resident_orbitals, BANDS_DEV, axis=0)
    kernel = coulomb(jnp.arange(NG, dtype=jnp.int32), jnp.arange(NG, dtype=jnp.int32),
                     jnp.arange(NG // 2 + 1, dtype=jnp.int32), NG)
    band_ids = jnp.arange(BANDS_DEV, dtype=jnp.int32)

    def one_block(inputs):
        own_block, resident_block, received_block, list_block, count_block = inputs
        running_sum = jnp.zeros(own_block.shape, jnp.float32)
        for list_index, partners in ((0, resident_block), (1, received_block)):
            for slot_index in range(PAIRS):
                first_band = list_block[list_index, slot_index, 0]
                second_band = list_block[list_index, slot_index, 1]
                partner_row = lax.dynamic_index_in_dim(partners, second_band, 0, keepdims=False).astype(jnp.float32)
                own_row = lax.dynamic_index_in_dim(own_block, first_band, 0, keepdims=False).astype(jnp.float32)
                potential = poisson(own_row * partner_row, kernel)
                live_weight = (slot_index < count_block[list_index]).astype(jnp.float32)
                weights = (band_ids == first_band).astype(jnp.float32) * live_weight
                running_sum = running_sum + weights[:, None, None, None] * (potential * partner_row)[None]
        intersection = jnp.dot(own_block.reshape(BANDS_DEV, -1).astype(jnp.float32),
                          running_sum.reshape(BANDS_DEV, -1).T, precision=lax.Precision.HIGHEST)
        return running_sum.astype(jnp.bfloat16), intersection

    shape_blocks = (BLOCKS, BANDS_DEV, NG, NG, NG)
    exchange_all, intersection_all = lax.map(one_block, (own_orbitals.reshape(shape_blocks),
                                                    resident_orbitals.reshape(shape_blocks),
                                                    received.reshape(shape_blocks),
                                                    pair_lists, pair_counts))
    return exchange_all.reshape(BANDS, NG, NG, NG), intersection_all.reshape(BANDS, BANDS_DEV)
```

```python
import functools
import math

import jax
import jax.numpy as jnp
import numpy as np
from jax import lax
from jax.experimental import pallas as pl
from jax.experimental.pallas import tpu as pltpu
from jax.sharding import PartitionSpec as P

BF16 = jnp.bfloat16
F32 = jnp.float32
TOP = 32766.0
STEPS = 256.0


def passed_along(x, axis, by):
    length = lax.axis_size(axis)
    return lax.ppermute(x, axis, [(i, (i + by) % length) for i in range(length)])


def cas_halves(length):
    indices = np.arange(length)
    angles = (indices[:, None] * indices[None, :] % length) * (2.0 * math.pi / length)
    table = (np.cos(angles) + np.sin(angles)) / math.sqrt(length)
    high = table.astype(np.float32).astype(BF16)
    low = (table - high.astype(np.float64)).astype(np.float32).astype(BF16)
    return high, low


def right_table(length):
    high, low = cas_halves(length)
    row = np.concatenate([high, low], axis=1)
    return np.concatenate([row, row], axis=0)


def left_table(length):
    high, low = cas_halves(length)
    column = np.concatenate([high, low], axis=0)
    return np.concatenate([column, column], axis=1)


def halves(x):
    high = x.astype(BF16)
    return high, (x - high.astype(F32)).astype(BF16)


def from_right(x, table):
    half = x.shape[1]
    both = jnp.dot(jnp.concatenate(halves(x), axis=1), table, preferred_element_type=F32)
    return both[:, :half] + both[:, half:]


def from_left(x, table):
    half = x.shape[0]
    both = jnp.dot(table, jnp.concatenate(halves(x), axis=0), preferred_element_type=F32)
    return both[:half] + both[half:]


def scale_code(peak):
    return jnp.ceil(jnp.log2(jnp.maximum(peak, 1e-37)) * STEPS)


def decoded_scale(code):
    return jnp.exp2(code * (1.0 / STEPS)) * (1.0 / TOP)


def encode(load, store, planes, carry):
    values = [load(plane) for plane in range(planes)]
    peak = functools.reduce(jnp.maximum, [jnp.abs(value) for value in values])
    code = scale_code(peak)
    inverse = jnp.exp2(code * (-1.0 / STEPS)) * TOP
    left = None
    for plane, value in enumerate(values):
        scaled = value * inverse
        if left is not None:
            scaled = scaled + left
        whole = jnp.round(scaled)
        if carry:
            left = scaled - whole
        store(plane, whole.astype(jnp.int32).astype(jnp.int16))
    store(planes, code.astype(jnp.int32).astype(jnp.int16))


def slot_table(lists_ref, counts_ref, slots):
    table = []
    for slot in range(slots):
        if slot < 2:
            which, place = slot, 0
        elif slots == 3:
            which, place = jnp.where(counts_ref[0] == 2, 0, 1), 1
        else:
            which, place = slot - 2, 1
        base = (which * 2 + place) * 2
        table.append((which, lists_ref[base], lists_ref[base + 1]))
    return table


def partner_plane(resident_ref, received_ref, which, band, plane):
    if isinstance(which, int):
        chosen = received_ref if which else resident_ref
        return chosen[band, plane].astype(F32)
    return jnp.where(
        which == 1, received_ref[band, plane].astype(F32), resident_ref[band, plane].astype(F32)
    )


def forward_kernel(
    slots, lists_ref, counts_ref, own_ref, resident_ref, received_ref, right_ref, left_ref, out_ref, field
):
    table = slot_table(lists_ref, counts_ref, slots)
    planes = own_ref.shape[1]
    pieces, rows = out_ref.shape[0], out_ref.shape[3]
    for slot, (which, first, second) in enumerate(table):

        @pl.loop(0, planes // 2)
        def _(pair):
            densities = []
            for side in range(2):
                plane = pair * 2 + side
                partner = partner_plane(resident_ref, received_ref, which, second, plane)
                densities.append(own_ref[first, plane].astype(F32) * partner)
            lines = from_right(jnp.concatenate(densities, axis=0), right_ref[...])
            length = lines.shape[1]
            lines = jnp.concatenate([lines[:length], lines[length:]], axis=1)
            lines = from_left(lines, left_ref[...])
            for side in range(2):
                field[pair * 2 + side] = lines[:, side * length : (side + 1) * length]

        @pl.loop(0, pieces)
        def _(piece):
            start = pl.multiple_of(piece * rows, rows)

            def store(plane, value):
                out_ref[piece, slot, plane] = value

            encode(lambda plane: field[plane, pl.ds(start, rows), :], store, planes, True)


def middle_kernel(slots, place_ref, got_ref, left_ref, out_ref, before, after):
    pieces, rows = got_ref.shape[0], got_ref.shape[3]
    planes = got_ref.shape[2] - 1
    length = pieces * planes
    first = lax.broadcasted_iota(jnp.int32, (length, length), 0)
    last = lax.broadcasted_iota(jnp.int32, (length, length), 1)
    first = jnp.minimum(first, length - first).astype(F32)
    last = jnp.minimum(last, length - last).astype(F32)
    around = first * first + last * last
    for slot in range(slots):

        @pl.loop(0, pieces)
        def _(piece):
            scale = decoded_scale(got_ref[piece, slot, planes].astype(jnp.int32).astype(F32))
            for plane in range(planes):
                start = pl.multiple_of(piece * planes * rows, planes * rows) + plane * rows
                before[slot, pl.ds(pl.multiple_of(start, rows), rows), :] = (
                    got_ref[piece, slot, plane].astype(jnp.int32).astype(F32) * scale
                )

    for pair in range(rows // 2):
        kernels = []
        for side in range(2):
            middle = place_ref[0] * rows + pair * 2 + side
            middle = jnp.minimum(middle, length - middle).astype(F32)
            squared = around + middle * middle
            kernels.append(
                jnp.where(squared > 0.5, 0.25 * length**1.5 / jnp.maximum(squared, 1.0), 0.0)
            )
        kernels = jnp.concatenate(kernels, axis=1)
        for slot in range(slots):
            lines = jnp.concatenate(
                [before[slot, pl.ds(pair * 2 + side, length, stride=rows), :] for side in range(2)],
                axis=1,
            )
            lines = from_left(lines, left_ref[...]) * kernels
            lines = from_left(lines, left_ref[...])
            for side in range(2):
                after[slot, pl.ds(pair * 2 + side, length, stride=rows), :] = lines[
                    :, side * length : (side + 1) * length
                ]

    for slot in range(slots):

        @pl.loop(0, pieces)
        def _(piece):
            def load(plane):
                start = pl.multiple_of(piece * planes * rows, planes * rows) + plane * rows
                return after[slot, pl.ds(pl.multiple_of(start, rows), rows), :]

            def store(plane, value):
                out_ref[piece, slot, plane] = value

            encode(load, store, planes, False)


def final_kernel(
    slots,
    lists_ref,
    counts_ref,
    own_ref,
    resident_ref,
    received_ref,
    got_ref,
    right_ref,
    left_ref,
    out_ref,
    terms_ref,
    scales,
    sums,
):
    table = slot_table(lists_ref, counts_ref, slots)
    bands, planes = own_ref.shape[0], own_ref.shape[1]
    pieces, rows = got_ref.shape[0], got_ref.shape[3]
    length = pieces * rows
    for slot in range(slots):
        code = got_ref[:, slot, planes].astype(jnp.int32).astype(F32).reshape(length, length)
        scales[slot] = decoded_scale(code)
    sums[...] = jnp.zeros_like(sums)

    @pl.loop(0, planes // 2)
    def _(pair):
        totals = [[jnp.zeros((length, length), F32) for _ in range(bands)] for _ in range(2)]
        for slot, (which, first, second) in enumerate(table):
            lines = []
            for side in range(2):
                value = got_ref[:, slot, pair * 2 + side].astype(jnp.int32).astype(F32)
                lines.append(value.reshape(length, length) * scales[slot])
            lines = from_left(jnp.concatenate(lines, axis=1), left_ref[...])
            lines = jnp.concatenate([lines[:, :length], lines[:, length:]], axis=0)
            lines = from_right(lines, right_ref[...])
            for side in range(2):
                plane = pair * 2 + side
                term = lines[side * length : (side + 1) * length] * partner_plane(
                    resident_ref, received_ref, which, second, plane
                )
                for band in range(bands):
                    totals[side][band] += jnp.where(first == band, term, 0.0)
        for side in range(2):
            plane = pair * 2 + side
            for band in range(bands):
                out_ref[band, plane] = totals[side][band].astype(out_ref.dtype)
                for other in range(bands):
                    product = own_ref[other, plane].astype(F32) * totals[side][band]
                    sums[other * bands + band] += product.reshape(length // 8, 8, length).sum(axis=0)

    for entry in range(bands * bands):
        row = jnp.sum(sums[entry], axis=0, keepdims=True)
        terms_ref[:, entry : entry + 1, :] = jnp.broadcast_to(
            row[None], (terms_ref.shape[0], 1, row.shape[1])
        )


VMEM = pl.BlockSpec(memory_space=pltpu.VMEM)
SMEM = pl.BlockSpec(memory_space=pltpu.SMEM)


def on_device(right, left, own_orbitals, resident_orbitals, pair_lists, pair_counts):
    bands, planes, length = own_orbitals.shape[:3]
    pieces = lax.axis_size("grid")
    rows = length // pieces
    place = lax.axis_index("grid").astype(jnp.int32).reshape(1)
    received = passed_along(resident_orbitals, "band", 1)
    lists = pair_lists.reshape(-1)
    counts = pair_counts.reshape(-1)

    def branch(slots):
        coded = jax.ShapeDtypeStruct((pieces, slots, planes + 1, rows, length), jnp.int16)

        def run(own_orbitals, resident_orbitals, received, lists, counts, place, right, left):
            sent = pl.pallas_call(
                functools.partial(forward_kernel, slots),
                out_shape=coded,
                in_specs=[SMEM, SMEM, VMEM, VMEM, VMEM, VMEM, VMEM],
                out_specs=VMEM,
                scratch_shapes=[pltpu.VMEM((planes, length, length), F32)],
                name="forward",
            )(lists, counts, own_orbitals, resident_orbitals, received, right, left)
            got = lax.all_to_all(sent, "grid", split_axis=0, concat_axis=0, tiled=True)
            sent = pl.pallas_call(
                functools.partial(middle_kernel, slots),
                out_shape=coded,
                in_specs=[SMEM, VMEM, VMEM],
                out_specs=VMEM,
                scratch_shapes=[pltpu.VMEM((slots, length * rows, length), F32)] * 2,
                name="middle",
            )(place, got, left)
            got = lax.all_to_all(sent, "grid", split_axis=0, concat_axis=0, tiled=True)
            return pl.pallas_call(
                functools.partial(final_kernel, slots),
                out_shape=(
                    jax.ShapeDtypeStruct(own_orbitals.shape, BF16),
                    jax.ShapeDtypeStruct((pieces, bands * bands, length), F32),
                ),
                in_specs=[SMEM, SMEM, VMEM, VMEM, VMEM, VMEM, VMEM, VMEM],
                out_specs=(VMEM, VMEM),
                scratch_shapes=[
                    pltpu.VMEM((slots, length, length), F32),
                    pltpu.VMEM((bands * bands, 8, length), F32),
                ],
                name="final",
            )(lists, counts, own_orbitals, resident_orbitals, received, got, right, left)

        return run

    exchange, terms = lax.switch(
        counts[0] + counts[1] - 2,
        [branch(2), branch(3), branch(4)],
        own_orbitals,
        resident_orbitals,
        received,
        lists,
        counts,
        place,
        right,
        left,
    )
    terms = lax.all_to_all(terms, "grid", split_axis=0, concat_axis=0, tiled=True)
    intersection = jnp.sum(terms, axis=(0, 2)).reshape(bands, bands)
    return exchange, intersection


def solution(mesh):
    in_specs = (
        P(None, None),
        P(None, None),
        P("band", "grid", None, None),
        P("band", "grid", None, None),
        P("band", None, None, None),
        P("band", None),
    )
    out_specs = (P("band", "grid", None, None), P("band", None))
    mapped = jax.shard_map(
        on_device, mesh=mesh, in_specs=in_specs, out_specs=out_specs, check_vma=False
    )

    def step(own_orbitals, resident_orbitals, pair_lists, pair_counts):
        length = own_orbitals.shape[-1]
        right, left = jnp.asarray(right_table(length)), jnp.asarray(left_table(length))
        return mapped(right, left, own_orbitals, resident_orbitals, pair_lists, pair_counts)

    return step
```

```python
import functools
import math

import jax
import jax.numpy as jnp
import numpy as np
from jax import lax
from jax.experimental import pallas as pl
from jax.experimental.pallas import tpu as pltpu
from jax.sharding import PartitionSpec as P

BF16 = jnp.bfloat16
F32 = jnp.float32
TOP = 32766.0
STEPS = 256.0
GROUP = 4


def passed_along(x, axis, by):
    length = lax.axis_size(axis)
    return lax.ppermute(x, axis, [(i, (i + by) % length) for i in range(length)])


def cas_halves(length):
    indices = np.arange(length)
    angles = (indices[:, None] * indices[None, :] % length) * (2.0 * math.pi / length)
    table = (np.cos(angles) + np.sin(angles)) / math.sqrt(length)
    high = table.astype(np.float32).astype(BF16)
    low = (table - high.astype(np.float64)).astype(np.float32).astype(BF16)
    return high, low


def right_table(length):
    high, low = cas_halves(length)
    row = np.concatenate([high, low], axis=1)
    return np.concatenate([row, row], axis=0)


def left_table(length):
    high, low = cas_halves(length)
    column = np.concatenate([high, low], axis=0)
    return np.concatenate([column, column], axis=1)


def halves(x):
    high = x.astype(BF16)
    return high, (x - high.astype(F32)).astype(BF16)


def from_right(x, table):
    half = x.shape[1]
    both = jnp.dot(jnp.concatenate(halves(x), axis=1), table, preferred_element_type=F32)
    return both[:, :half] + both[:, half:]


def from_left(x, table):
    half = x.shape[0]
    both = jnp.dot(table, jnp.concatenate(halves(x), axis=0), preferred_element_type=F32)
    return both[:half] + both[half:]


def scale_code(peak):
    return jnp.ceil(jnp.log2(jnp.maximum(peak, 1e-37)) * STEPS)


def decoded_scale(code):
    return jnp.exp2(code * (1.0 / STEPS)) * (1.0 / TOP)


def encode(load, store, planes, carry):
    values = [load(plane) for plane in range(planes)]
    peak = functools.reduce(jnp.maximum, [jnp.abs(value) for value in values])
    code = scale_code(peak)
    inverse = jnp.exp2(code * (-1.0 / STEPS)) * TOP
    left = None
    for plane, value in enumerate(values):
        scaled = value * inverse
        if left is not None:
            scaled = scaled + left
        whole = jnp.round(scaled)
        if carry:
            left = scaled - whole
        store(plane, whole.astype(jnp.int32))
    store(planes, code.astype(jnp.int32))


def store_coded(out_ref, piece, slot, rows):
    def store(plane, value):
        count = value.shape[0] // rows
        value = value.reshape(count, rows, value.shape[1]).astype(jnp.int16)
        out_ref[pl.ds(piece, count), slot, plane] = value

    return store


def forward_slot(own_ref, first, partner_ref, second, right_ref, left_ref, out_ref, slot, field):
    planes, length = own_ref.shape[1], own_ref.shape[2]
    pieces, rows = out_ref.shape[0], out_ref.shape[3]
    for pair in range(planes // 2):
        densities = [
            own_ref[first, plane].astype(F32) * partner_ref[second, plane].astype(F32)
            for plane in (pair * 2, pair * 2 + 1)
        ]
        lines = from_right(jnp.concatenate(densities, axis=0), right_ref[...])
        lines = jnp.concatenate([lines[:length], lines[length:]], axis=1)
        lines = from_left(lines, left_ref[...])
        for side in range(2):
            field[pair * 2 + side] = lines[:, side * length : (side + 1) * length]
    for piece in range(0, pieces, GROUP):
        encode(
            lambda plane: field[plane, pl.ds(piece * rows, GROUP * rows), :],
            store_coded(out_ref, piece, slot, rows),
            planes,
            True,
        )


def early_kernel(
    lists_ref, counts_ref, place_ref, own_ref, resident_ref, right_ref, left_ref, out_ref, kernel_ref, field
):
    slots, rows, length = out_ref.shape[1], out_ref.shape[3], out_ref.shape[4]
    for slot in range(slots):

        @pl.when(slot < counts_ref[0])
        def _():
            forward_slot(
                own_ref,
                lists_ref[slot * 2],
                resident_ref,
                lists_ref[slot * 2 + 1],
                right_ref,
                left_ref,
                out_ref,
                slot,
                field,
            )

    first = lax.broadcasted_iota(jnp.int32, (length, length), 0)
    last = lax.broadcasted_iota(jnp.int32, (length, length), 1)
    first = jnp.minimum(first, length - first).astype(F32)
    last = jnp.minimum(last, length - last).astype(F32)
    around = first * first + last * last
    for row in range(rows):
        middle = place_ref[0] * rows + row
        middle = jnp.minimum(middle, length - middle).astype(F32)
        squared = around + middle * middle
        kernel_ref[:, row * length : (row + 1) * length] = jnp.where(
            squared > 0.5, 0.25 * length**1.5 / jnp.maximum(squared, 1.0), 0.0
        )


def late_kernel(
    slots, lists_ref, counts_ref, own_ref, received_ref, early_ref, right_ref, left_ref, out_ref, field
):
    place = early_ref.shape[1] * 2

    def transform(number, slot):
        forward_slot(
            own_ref,
            lists_ref[place + number * 2],
            received_ref,
            lists_ref[place + number * 2 + 1],
            right_ref,
            left_ref,
            out_ref,
            slot,
            field,
        )

    out_ref[:, 0] = early_ref[:, 0]
    transform(0, 1)
    if slots == 3:

        @pl.when(counts_ref[0] == 2)
        def _():
            out_ref[:, 2] = early_ref[:, 1]

        @pl.when(counts_ref[0] != 2)
        def _():
            transform(1, 2)

    if slots == 4:
        out_ref[:, 2] = early_ref[:, 1]
        transform(1, 3)


def middle_kernel(slots, got_ref, kernel_ref, left_ref, out_ref, before, after):
    pieces, rows = got_ref.shape[0], got_ref.shape[3]
    planes = got_ref.shape[2] - 1
    length = pieces * planes
    for slot in range(slots):
        for piece in range(pieces):
            scale = decoded_scale(got_ref[piece, slot, planes].astype(jnp.int32).astype(F32))
            for plane in range(planes):
                start = (piece * planes + plane) * rows
                before[slot, pl.ds(start, rows), :] = (
                    got_ref[piece, slot, plane].astype(jnp.int32).astype(F32) * scale
                )
        for pair in range(rows // 2):
            lines = jnp.concatenate(
                [before[slot, pl.ds(pair * 2 + side, length, stride=rows), :] for side in range(2)],
                axis=1,
            )
            lines = from_left(lines, left_ref[...])
            lines = lines * kernel_ref[:, pair * 2 * length : (pair + 1) * 2 * length]
            lines = from_left(lines, left_ref[...])
            for side in range(2):
                after[slot, pl.ds(pair * 2 + side, length, stride=rows), :] = lines[
                    :, side * length : (side + 1) * length
                ]
        for piece in range(pieces):
            encode(
                lambda plane: after[slot, pl.ds((piece * planes + plane) * rows, rows), :],
                store_coded(out_ref, piece, slot, rows),
                planes,
                False,
            )


def slot_table(lists_ref, counts_ref, slots):
    table = []
    for slot in range(slots):
        if slot < 2:
            which, place = slot, 0
        elif slots == 3:
            which, place = jnp.where(counts_ref[0] == 2, 0, 1), 1
        else:
            which, place = slot - 2, 1
        base = (which * 2 + place) * 2
        table.append((which, lists_ref[base], lists_ref[base + 1]))
    return table


def partner_plane(resident_ref, received_ref, which, band, plane):
    if isinstance(which, int):
        chosen = received_ref if which else resident_ref
        return chosen[band, plane].astype(F32)
    return jnp.where(
        which == 1, received_ref[band, plane].astype(F32), resident_ref[band, plane].astype(F32)
    )


def final_kernel(
    slots,
    lists_ref,
    counts_ref,
    own_ref,
    resident_ref,
    received_ref,
    got_ref,
    right_ref,
    left_ref,
    out_ref,
    terms_ref,
    scales,
    sums,
):
    table = slot_table(lists_ref, counts_ref, slots)
    bands, planes = own_ref.shape[0], own_ref.shape[1]
    pieces, rows = got_ref.shape[0], got_ref.shape[3]
    length = pieces * rows
    for slot in range(slots):
        code = got_ref[:, slot, planes].astype(jnp.int32).astype(F32).reshape(length, length)
        scales[slot] = decoded_scale(code)
    sums[...] = jnp.zeros_like(sums)
    for pair in range(planes // 2):
        totals = [[jnp.zeros((length, length), F32) for _ in range(bands)] for _ in range(2)]
        for slot, (which, first, second) in enumerate(table):
            lines = []
            for side in range(2):
                value = got_ref[:, slot, pair * 2 + side].astype(jnp.int32).astype(F32)
                lines.append(value.reshape(length, length) * scales[slot])
            lines = from_left(jnp.concatenate(lines, axis=1), left_ref[...])
            lines = jnp.concatenate([lines[:, :length], lines[:, length:]], axis=0)
            lines = from_right(lines, right_ref[...])
            for side in range(2):
                plane = pair * 2 + side
                term = lines[side * length : (side + 1) * length] * partner_plane(
                    resident_ref, received_ref, which, second, plane
                )
                for band in range(bands):
                    totals[side][band] += jnp.where(first == band, term, 0.0)
        for side in range(2):
            plane = pair * 2 + side
            for band in range(bands):
                out_ref[band, plane] = totals[side][band].astype(out_ref.dtype)
                for other in range(bands):
                    product = own_ref[other, plane].astype(F32) * totals[side][band]
                    sums[other * bands + band] += product.reshape(length // 8, 8, length).sum(axis=0)

    for entry in range(bands * bands):
        row = jnp.sum(sums[entry], axis=0, keepdims=True)
        terms_ref[:, entry // bands, entry % bands : entry % bands + 1, :] = jnp.broadcast_to(
            row[None], (terms_ref.shape[0], 1, row.shape[1])
        )


VMEM = pl.BlockSpec(memory_space=pltpu.VMEM)
SMEM = pl.BlockSpec(memory_space=pltpu.SMEM)


def on_device(right, left, own_orbitals, resident_orbitals, pair_lists, pair_counts):
    bands, planes, length = own_orbitals.shape[:3]
    pieces = lax.axis_size("grid")
    rows = length // pieces
    place = lax.axis_index("grid").astype(jnp.int32).reshape(1)
    received = passed_along(resident_orbitals, "band", 1)
    lists = pair_lists.reshape(-1)
    counts = pair_counts.reshape(-1)
    field = pltpu.VMEM((planes, length, length), F32)

    def coded(slots):
        return jax.ShapeDtypeStruct((pieces, slots, planes + 1, rows, length), jnp.int16)

    early, kernel = pl.pallas_call(
        early_kernel,
        out_shape=(coded(2), jax.ShapeDtypeStruct((length, rows * length), F32)),
        in_specs=[SMEM, SMEM, SMEM, VMEM, VMEM, VMEM, VMEM],
        out_specs=(VMEM, VMEM),
        scratch_shapes=[field],
        cost_estimate=pl.CostEstimate(
            flops=600_000_000, bytes_accessed=3_000_000, transcendentals=0
        ),
        name="early",
    )(lists, counts, place, own_orbitals, resident_orbitals, right, left)

    def branch(slots):
        def run(own_orbitals, resident_orbitals, received, lists, counts, early, kernel, right, left):
            sent = pl.pallas_call(
                functools.partial(late_kernel, slots),
                out_shape=coded(slots),
                in_specs=[SMEM, SMEM, VMEM, VMEM, VMEM, VMEM, VMEM],
                out_specs=VMEM,
                scratch_shapes=[field],
                name="late",
            )(lists, counts, own_orbitals, received, early, right, left)
            got = lax.all_to_all(sent, "grid", split_axis=0, concat_axis=0, tiled=True)
            sent = pl.pallas_call(
                functools.partial(middle_kernel, slots),
                out_shape=coded(slots),
                in_specs=[VMEM, VMEM, VMEM],
                out_specs=VMEM,
                scratch_shapes=[pltpu.VMEM((slots, length * rows, length), F32)] * 2,
                name="middle",
            )(got, kernel, left)
            got = lax.all_to_all(sent, "grid", split_axis=0, concat_axis=0, tiled=True)
            return pl.pallas_call(
                functools.partial(final_kernel, slots),
                out_shape=(
                    jax.ShapeDtypeStruct(own_orbitals.shape, BF16),
                    jax.ShapeDtypeStruct((pieces, bands, bands, length), F32),
                ),
                in_specs=[SMEM, SMEM, VMEM, VMEM, VMEM, VMEM, VMEM, VMEM],
                out_specs=(VMEM, VMEM),
                scratch_shapes=[
                    pltpu.VMEM((slots, length, length), F32),
                    pltpu.VMEM((bands * bands, 8, length), F32),
                ],
                name="final",
            )(lists, counts, own_orbitals, resident_orbitals, received, got, right, left)

        return run

    exchange, terms = lax.switch(
        counts[0] + counts[1] - 2,
        [branch(2), branch(3), branch(4)],
        own_orbitals,
        resident_orbitals,
        received,
        lists,
        counts,
        early,
        kernel,
        right,
        left,
    )
    terms = lax.all_to_all(terms, "grid", split_axis=0, concat_axis=0, tiled=True)
    return exchange, jnp.sum(terms, axis=(0, 3))


def solution(mesh):
    in_specs = (
        P(None, None),
        P(None, None),
        P("band", "grid", None, None),
        P("band", "grid", None, None),
        P("band", None, None, None),
        P("band", None),
    )
    out_specs = (P("band", "grid", None, None), P("band", None))
    mapped = jax.shard_map(
        on_device, mesh=mesh, in_specs=in_specs, out_specs=out_specs, check_vma=False
    )

    def step(own_orbitals, resident_orbitals, pair_lists, pair_counts):
        length = own_orbitals.shape[-1]
        right, left = jnp.asarray(right_table(length)), jnp.asarray(left_table(length))
        return mapped(right, left, own_orbitals, resident_orbitals, pair_lists, pair_counts)

    return step
```

```python
import functools
import math

import jax
import jax.numpy as jnp
import numpy as np
from jax import lax
from jax.experimental import pallas as pl
from jax.experimental.pallas import tpu as pltpu
from jax.sharding import PartitionSpec as P

BF16 = jnp.bfloat16
F32 = jnp.float32
TOP = 32766.0
STEPS = 256.0
GROUP = 4
LIMIT = pltpu.CompilerParams(vmem_limit_bytes=20 << 20)


def passed_along(x, axis, by):
    length = lax.axis_size(axis)
    return lax.ppermute(x, axis, [(i, (i + by) % length) for i in range(length)])


def cas_halves(length):
    indices = np.arange(length)
    angles = (indices[:, None] * indices[None, :] % length) * (2.0 * math.pi / length)
    table = (np.cos(angles) + np.sin(angles)) / math.sqrt(length)
    high = table.astype(np.float32).astype(BF16)
    low = (table - high.astype(np.float64)).astype(np.float32).astype(BF16)
    return high, low


def right_table(length):
    high, low = cas_halves(length)
    row = np.concatenate([high, low], axis=1)
    return np.concatenate([row, row], axis=0)


def left_table(length):
    high, low = cas_halves(length)
    column = np.concatenate([high, low], axis=0)
    return np.concatenate([column, column], axis=1)


def halves(x):
    high = x.astype(BF16)
    return high, (x - high.astype(F32)).astype(BF16)


def from_right(x, table):
    half = x.shape[1]
    both = jnp.dot(jnp.concatenate(halves(x), axis=1), table, preferred_element_type=F32)
    return both[:, :half] + both[:, half:]


def from_left(x, table):
    half = x.shape[0]
    both = jnp.dot(table, jnp.concatenate(halves(x), axis=0), preferred_element_type=F32)
    return both[:half] + both[half:]


def scale_code(peak):
    return jnp.ceil(jnp.log2(jnp.maximum(peak, 1e-37)) * STEPS)


def decoded_scale(code):
    return jnp.exp2(code * (1.0 / STEPS)) * (1.0 / TOP)


def encode(load, store, planes, carry):
    values = [load(plane) for plane in range(planes)]
    peak = functools.reduce(jnp.maximum, [jnp.abs(value) for value in values])
    code = scale_code(peak)
    inverse = jnp.exp2(code * (-1.0 / STEPS)) * TOP
    left = None
    for plane, value in enumerate(values):
        scaled = value * inverse
        if left is not None:
            scaled = scaled + left
        whole = jnp.round(scaled)
        if carry:
            left = scaled - whole
        store(plane, whole.astype(jnp.int32))
    store(planes, code.astype(jnp.int32))


def store_coded(out_ref, piece, slot, rows):
    def store(plane, value):
        count = value.shape[0] // rows
        value = value.reshape(count, rows, value.shape[1]).astype(jnp.int16)
        out_ref[pl.ds(piece, count), slot, plane] = value

    return store


def forward_slot(own_ref, first, partner_ref, second, right_ref, left_ref, out_ref, slot, field):
    planes, length = own_ref.shape[1], own_ref.shape[2]
    pieces, rows = out_ref.shape[0], out_ref.shape[3]
    for pair in range(planes // 2):
        densities = [
            own_ref[first, plane].astype(F32) * partner_ref[second, plane].astype(F32)
            for plane in (pair * 2, pair * 2 + 1)
        ]
        lines = from_right(jnp.concatenate(densities, axis=0), right_ref[...])
        lines = jnp.concatenate([lines[:length], lines[length:]], axis=1)
        lines = from_left(lines, left_ref[...])
        for side in range(2):
            field[pair * 2 + side] = lines[:, side * length : (side + 1) * length]
    for piece in range(0, pieces, GROUP):
        encode(
            lambda plane: field[plane, pl.ds(piece * rows, GROUP * rows), :],
            store_coded(out_ref, piece, slot, rows),
            planes,
            True,
        )


def early_kernel(
    lists_ref, counts_ref, place_ref, own_ref, resident_ref, right_ref, left_ref, out_ref, kernel_ref, field
):
    slots, rows, length = out_ref.shape[1], out_ref.shape[3], out_ref.shape[4]
    for slot in range(slots):

        @pl.when(slot < counts_ref[0])
        def _():
            forward_slot(
                own_ref,
                lists_ref[slot * 2],
                resident_ref,
                lists_ref[slot * 2 + 1],
                right_ref,
                left_ref,
                out_ref,
                slot,
                field,
            )

    first = lax.broadcasted_iota(jnp.int32, (length, length), 0)
    last = lax.broadcasted_iota(jnp.int32, (length, length), 1)
    first = jnp.minimum(first, length - first).astype(F32)
    last = jnp.minimum(last, length - last).astype(F32)
    around = first * first + last * last
    for row in range(rows):
        middle = place_ref[0] * rows + row
        middle = jnp.minimum(middle, length - middle).astype(F32)
        squared = around + middle * middle
        kernel_ref[:, row * length : (row + 1) * length] = jnp.where(
            squared > 0.5, 0.25 * length**1.5 / jnp.maximum(squared, 1.0), 0.0
        )


def late_kernel(
    slots, lists_ref, counts_ref, own_ref, received_ref, early_ref, right_ref, left_ref, out_ref, field
):
    place = early_ref.shape[1] * 2

    def transform(number, slot):
        forward_slot(
            own_ref,
            lists_ref[place + number * 2],
            received_ref,
            lists_ref[place + number * 2 + 1],
            right_ref,
            left_ref,
            out_ref,
            slot,
            field,
        )

    out_ref[:, 0] = early_ref[:, 0]
    transform(0, 1)
    if slots == 3:

        @pl.when(counts_ref[0] == 2)
        def _():
            out_ref[:, 2] = early_ref[:, 1]

        @pl.when(counts_ref[0] != 2)
        def _():
            transform(1, 2)

    if slots == 4:
        out_ref[:, 2] = early_ref[:, 1]
        transform(1, 3)


def middle_kernel(slots, got_ref, kernel_ref, left_ref, out_ref, before, after):
    pieces, rows = got_ref.shape[0], got_ref.shape[3]
    planes = got_ref.shape[2] - 1
    length = pieces * planes
    for slot in range(slots):
        for piece in range(pieces):
            scale = decoded_scale(got_ref[piece, slot, planes].astype(jnp.int32).astype(F32))
            for plane in range(planes):
                start = (piece * planes + plane) * rows
                before[slot, pl.ds(start, rows), :] = (
                    got_ref[piece, slot, plane].astype(jnp.int32).astype(F32) * scale
                )
        for pair in range(rows // 2):
            lines = jnp.concatenate(
                [before[slot, pl.ds(pair * 2 + side, length, stride=rows), :] for side in range(2)],
                axis=1,
            )
            lines = from_left(lines, left_ref[...])
            lines = lines * kernel_ref[:, pair * 2 * length : (pair + 1) * 2 * length]
            lines = from_left(lines, left_ref[...])
            for side in range(2):
                after[slot, pl.ds(pair * 2 + side, length, stride=rows), :] = lines[
                    :, side * length : (side + 1) * length
                ]
        for piece in range(pieces):
            encode(
                lambda plane: after[slot, pl.ds((piece * planes + plane) * rows, rows), :],
                store_coded(out_ref, piece, slot, rows),
                planes,
                False,
            )


def slot_table(lists_ref, counts_ref, slots):
    table = []
    for slot in range(slots):
        if slot < 2:
            which, place = slot, 0
        elif slots == 3:
            which, place = jnp.where(counts_ref[0] == 2, 0, 1), 1
        else:
            which, place = slot - 2, 1
        base = (which * 2 + place) * 2
        table.append((which, lists_ref[base], lists_ref[base + 1]))
    return table


def partner_plane(resident_ref, received_ref, which, band, plane):
    if isinstance(which, int):
        chosen = received_ref if which else resident_ref
        return chosen[band, plane].astype(F32)
    return jnp.where(
        which == 1, received_ref[band, plane].astype(F32), resident_ref[band, plane].astype(F32)
    )


def final_kernel(
    slots,
    lists_ref,
    counts_ref,
    own_ref,
    resident_ref,
    received_ref,
    got_ref,
    right_ref,
    left_ref,
    out_ref,
    terms_ref,
    scales,
    sums,
):
    table = slot_table(lists_ref, counts_ref, slots)
    bands, planes = own_ref.shape[0], own_ref.shape[1]
    pieces, rows = got_ref.shape[0], got_ref.shape[3]
    length = pieces * rows
    for slot in range(slots):
        code = got_ref[:, slot, planes].astype(jnp.int32).astype(F32).reshape(length, length)
        scales[slot] = decoded_scale(code)
    sums[...] = jnp.zeros_like(sums)
    for pair in range(planes // 2):
        totals = [[jnp.zeros((length, length), F32) for _ in range(bands)] for _ in range(2)]
        for slot, (which, first, second) in enumerate(table):
            lines = []
            for side in range(2):
                value = got_ref[:, slot, pair * 2 + side].astype(jnp.int32).astype(F32)
                lines.append(value.reshape(length, length) * scales[slot])
            lines = from_left(jnp.concatenate(lines, axis=1), left_ref[...])
            lines = jnp.concatenate([lines[:, :length], lines[:, length:]], axis=0)
            lines = from_right(lines, right_ref[...])
            for side in range(2):
                plane = pair * 2 + side
                term = lines[side * length : (side + 1) * length] * partner_plane(
                    resident_ref, received_ref, which, second, plane
                )
                for band in range(bands):
                    totals[side][band] += jnp.where(first == band, term, 0.0)
        for side in range(2):
            plane = pair * 2 + side
            for band in range(bands):
                out_ref[band, plane] = totals[side][band].astype(out_ref.dtype)
                for other in range(bands):
                    product = own_ref[other, plane].astype(F32) * totals[side][band]
                    sums[other * bands + band] += product.reshape(length // 8, 8, length).sum(axis=0)

    for entry in range(bands * bands):
        row = jnp.sum(sums[entry], axis=0, keepdims=True)
        terms_ref[:, entry // bands, entry % bands : entry % bands + 1, :] = jnp.broadcast_to(
            row[None], (terms_ref.shape[0], 1, row.shape[1])
        )


VMEM = pl.BlockSpec(memory_space=pltpu.VMEM)
SMEM = pl.BlockSpec(memory_space=pltpu.SMEM)


def on_device(right, left, own_orbitals, resident_orbitals, pair_lists, pair_counts):
    bands, planes, length = own_orbitals.shape[:3]
    pieces = lax.axis_size("grid")
    rows = length // pieces
    place = lax.axis_index("grid").astype(jnp.int32).reshape(1)
    received = passed_along(resident_orbitals, "band", 1)
    lists = pair_lists.reshape(-1)
    counts = pair_counts.reshape(-1)
    field = pltpu.VMEM((planes, length, length), F32)

    def coded(slots):
        return jax.ShapeDtypeStruct((pieces, slots, planes + 1, rows, length), jnp.int16)

    early, kernel = pl.pallas_call(
        early_kernel,
        out_shape=(coded(2), jax.ShapeDtypeStruct((length, rows * length), F32)),
        in_specs=[SMEM, SMEM, SMEM, VMEM, VMEM, VMEM, VMEM],
        out_specs=(VMEM, VMEM),
        scratch_shapes=[field],
        cost_estimate=pl.CostEstimate(
            flops=600_000_000, bytes_accessed=3_000_000, transcendentals=0
        ),
        compiler_params=LIMIT,
                name="early",
    )(lists, counts, place, own_orbitals, resident_orbitals, right, left)

    def branch(slots):
        def run(own_orbitals, resident_orbitals, received, lists, counts, early, kernel, right, left):
            sent = pl.pallas_call(
                functools.partial(late_kernel, slots),
                out_shape=coded(slots),
                in_specs=[SMEM, SMEM, VMEM, VMEM, VMEM, VMEM, VMEM],
                out_specs=VMEM,
                scratch_shapes=[field],
                compiler_params=LIMIT,
                name="late",
            )(lists, counts, own_orbitals, received, early, right, left)
            got = lax.all_to_all(sent, "grid", split_axis=0, concat_axis=0, tiled=True)
            sent = pl.pallas_call(
                functools.partial(middle_kernel, slots),
                out_shape=coded(slots),
                in_specs=[VMEM, VMEM, VMEM],
                out_specs=VMEM,
                scratch_shapes=[pltpu.VMEM((slots, length * rows, length), F32)] * 2,
                compiler_params=LIMIT,
                name="middle",
            )(got, kernel, left)
            got = lax.all_to_all(sent, "grid", split_axis=0, concat_axis=0, tiled=True)
            return pl.pallas_call(
                functools.partial(final_kernel, slots),
                out_shape=(
                    jax.ShapeDtypeStruct(own_orbitals.shape, BF16),
                    jax.ShapeDtypeStruct((pieces, bands, bands, length), F32),
                ),
                in_specs=[SMEM, SMEM, VMEM, VMEM, VMEM, VMEM, VMEM, VMEM],
                out_specs=(VMEM, VMEM),
                scratch_shapes=[
                    pltpu.VMEM((slots, length, length), F32),
                    pltpu.VMEM((bands * bands, 8, length), F32),
                ],
                compiler_params=LIMIT,
                name="final",
            )(lists, counts, own_orbitals, resident_orbitals, received, got, right, left)

        return run

    exchange, terms = lax.switch(
        counts[0] + counts[1] - 2,
        [branch(2), branch(3), branch(4)],
        own_orbitals,
        resident_orbitals,
        received,
        lists,
        counts,
        early,
        kernel,
        right,
        left,
    )
    terms = lax.all_to_all(terms, "grid", split_axis=0, concat_axis=0, tiled=True)
    return exchange, jnp.sum(terms, axis=(0, 3))


def solution(mesh):
    in_specs = (
        P(None, None),
        P(None, None),
        P("band", "grid", None, None),
        P("band", "grid", None, None),
        P("band", None, None, None),
        P("band", None),
    )
    out_specs = (P("band", "grid", None, None), P("band", None))
    mapped = jax.shard_map(
        on_device, mesh=mesh, in_specs=in_specs, out_specs=out_specs, check_vma=False
    )

    def step(own_orbitals, resident_orbitals, pair_lists, pair_counts):
        length = own_orbitals.shape[-1]
        right, left = jnp.asarray(right_table(length)), jnp.asarray(left_table(length))
        return mapped(right, left, own_orbitals, resident_orbitals, pair_lists, pair_counts)

    return step
```

```python
import functools
import math

import jax
import jax.numpy as jnp
import numpy as np
from jax import lax
from jax.experimental import pallas as pl
from jax.experimental.pallas import tpu as pltpu
from jax.sharding import PartitionSpec as P

BF16 = jnp.bfloat16
F32 = jnp.float32
TOP = 32766.0
STEPS = 256.0
GROUP = 4
LIMIT = pltpu.CompilerParams(vmem_limit_bytes=20 << 20)


def passed_along(x, axis, by):
    length = lax.axis_size(axis)
    return lax.ppermute(x, axis, [(i, (i + by) % length) for i in range(length)])


def cas_halves(length):
    indices = np.arange(length)
    angles = (indices[:, None] * indices[None, :] % length) * (2.0 * math.pi / length)
    table = (np.cos(angles) + np.sin(angles)) / math.sqrt(length)
    high = table.astype(np.float32).astype(BF16)
    low = (table - high.astype(np.float64)).astype(np.float32).astype(BF16)
    return high, low


def right_table(length):
    high, low = cas_halves(length)
    row = np.concatenate([high, low], axis=1)
    return np.concatenate([row, row], axis=0)


def left_table(length):
    high, low = cas_halves(length)
    column = np.concatenate([high, low], axis=0)
    return np.concatenate([column, column], axis=1)


def halves(x):
    high = x.astype(BF16)
    return high, (x - high.astype(F32)).astype(BF16)


def from_right(x, table):
    half = x.shape[1]
    both = jnp.dot(jnp.concatenate(halves(x), axis=1), table, preferred_element_type=F32)
    return both[:, :half] + both[:, half:]


def from_left(x, table):
    half = x.shape[0]
    both = jnp.dot(table, jnp.concatenate(halves(x), axis=0), preferred_element_type=F32)
    return both[:half] + both[half:]


def scale_code(peak):
    return jnp.ceil(jnp.log2(jnp.maximum(peak, 1e-37)) * STEPS)


def decoded_scale(code):
    return jnp.exp2(code * (1.0 / STEPS)) * (1.0 / TOP)


def encode(load, store, planes, carry):
    values = [load(plane) for plane in range(planes)]
    peak = functools.reduce(jnp.maximum, [jnp.abs(value) for value in values])
    code = scale_code(peak)
    inverse = jnp.exp2(code * (-1.0 / STEPS)) * TOP
    left = None
    for plane, value in enumerate(values):
        scaled = value * inverse
        if left is not None:
            scaled = scaled + left
        whole = jnp.round(scaled)
        if carry:
            left = scaled - whole
        store(plane, whole.astype(jnp.int32))
    store(planes, code.astype(jnp.int32))


def store_coded(out_ref, piece, slot, rows):
    def store(plane, value):
        count = value.shape[0] // rows
        value = value.reshape(count, rows, value.shape[1]).astype(jnp.int16)
        out_ref[pl.ds(piece, count), slot, plane] = value

    return store


def forward_slot(own_ref, first, partner_ref, second, right_ref, left_ref, out_ref, slot, field):
    planes, length = own_ref.shape[1], own_ref.shape[2]
    pieces, rows = out_ref.shape[0], out_ref.shape[3]
    for pair in range(planes // 2):
        densities = [
            own_ref[first, plane].astype(F32) * partner_ref[second, plane].astype(F32)
            for plane in (pair * 2, pair * 2 + 1)
        ]
        lines = from_right(jnp.concatenate(densities, axis=0), right_ref[...])
        lines = jnp.concatenate([lines[:length], lines[length:]], axis=1)
        lines = from_left(lines, left_ref[...])
        for side in range(2):
            field[pair * 2 + side] = lines[:, side * length : (side + 1) * length]
    for piece in range(0, pieces, GROUP):
        encode(
            lambda plane: field[plane, pl.ds(piece * rows, GROUP * rows), :],
            store_coded(out_ref, piece, slot, rows),
            planes,
            True,
        )


def early_kernel(
    lists_ref,
    counts_ref,
    own_hbm,
    resident_hbm,
    right_ref,
    left_ref,
    out_ref,
    kernel_ref,
    index_ref,
    field,
    own_ref,
    resident_ref,
    sems,
):
    slots, rows, length = out_ref.shape[1], out_ref.shape[3], out_ref.shape[4]
    copies = []
    for number, (source, target) in enumerate(((own_hbm, own_ref), (resident_hbm, resident_ref))):
        copy = pltpu.make_async_copy(source, target, sems.at[number])
        copy.start()
        copies.append(copy)
    index_ref[0] = counts_ref[0, 0] + counts_ref[0, 1] - 2
    place = lax.axis_index("grid")
    first = lax.broadcasted_iota(jnp.int32, (length, length), 0)
    last = lax.broadcasted_iota(jnp.int32, (length, length), 1)
    first = jnp.minimum(first, length - first).astype(F32)
    last = jnp.minimum(last, length - last).astype(F32)
    around = first * first + last * last
    for row in range(rows):
        middle = place * rows + row
        middle = jnp.minimum(middle, length - middle).astype(F32)
        squared = around + middle * middle
        kernel_ref[:, row * length : (row + 1) * length] = jnp.where(
            squared > 0.5, 0.25 * length**1.5 / jnp.maximum(squared, 1.0), 0.0
        )
    for copy in copies:
        copy.wait()

    def transform(slot):
        forward_slot(
            own_ref,
            lists_ref[0, 0, slot, 0],
            resident_ref,
            lists_ref[0, 0, slot, 1],
            right_ref,
            left_ref,
            out_ref,
            slot,
            field,
        )

    transform(0)
    for slot in range(1, slots):

        @pl.when(slot < counts_ref[0, 0])
        def _():
            transform(slot)


def late_kernel(
    slots, lists_ref, counts_ref, own_ref, received_ref, early_ref, right_ref, left_ref, out_ref, field
):
    def transform(number, slot):
        forward_slot(
            own_ref,
            lists_ref[0, 1, number, 0],
            received_ref,
            lists_ref[0, 1, number, 1],
            right_ref,
            left_ref,
            out_ref,
            slot,
            field,
        )

    out_ref[:, 0] = early_ref[:, 0]
    transform(0, 1)
    if slots == 3:

        @pl.when(counts_ref[0, 0] == 2)
        def _():
            out_ref[:, 2] = early_ref[:, 1]

        @pl.when(counts_ref[0, 0] != 2)
        def _():
            transform(1, 2)

    if slots == 4:
        out_ref[:, 2] = early_ref[:, 1]
        transform(1, 3)


def middle_kernel(slots, got_ref, kernel_ref, left_ref, out_ref, before, after):
    pieces, rows = got_ref.shape[0], got_ref.shape[3]
    planes = got_ref.shape[2] - 1
    length = pieces * planes
    for slot in range(slots):
        for piece in range(pieces):
            scale = decoded_scale(got_ref[piece, slot, planes].astype(jnp.int32).astype(F32))
            for plane in range(planes):
                start = (piece * planes + plane) * rows
                before[slot, pl.ds(start, rows), :] = (
                    got_ref[piece, slot, plane].astype(jnp.int32).astype(F32) * scale
                )
        for pair in range(rows // 2):
            lines = jnp.concatenate(
                [before[slot, pl.ds(pair * 2 + side, length, stride=rows), :] for side in range(2)],
                axis=1,
            )
            lines = from_left(lines, left_ref[...])
            lines = lines * kernel_ref[:, pair * 2 * length : (pair + 1) * 2 * length]
            lines = from_left(lines, left_ref[...])
            for side in range(2):
                after[slot, pl.ds(pair * 2 + side, length, stride=rows), :] = lines[
                    :, side * length : (side + 1) * length
                ]
        for piece in range(pieces):
            encode(
                lambda plane: after[slot, pl.ds((piece * planes + plane) * rows, rows), :],
                store_coded(out_ref, piece, slot, rows),
                planes,
                False,
            )


def slot_table(lists_ref, counts_ref, slots):
    table = []
    for slot in range(slots):
        if slot < 2:
            which, place = slot, 0
        elif slots == 3:
            which, place = jnp.where(counts_ref[0, 0] == 2, 0, 1), 1
        else:
            which, place = slot - 2, 1
        table.append((which, lists_ref[0, which, place, 0], lists_ref[0, which, place, 1]))
    return table


def partner_plane(resident_ref, received_ref, which, band, plane):
    if isinstance(which, int):
        chosen = received_ref if which else resident_ref
        return chosen[band, plane].astype(F32)
    return jnp.where(
        which == 1, received_ref[band, plane].astype(F32), resident_ref[band, plane].astype(F32)
    )


def final_kernel(
    slots,
    lists_ref,
    counts_ref,
    own_ref,
    resident_ref,
    received_ref,
    got_ref,
    right_ref,
    left_ref,
    out_ref,
    terms_ref,
    scales,
    sums,
):
    table = slot_table(lists_ref, counts_ref, slots)
    bands, planes = own_ref.shape[0], own_ref.shape[1]
    pieces, rows = got_ref.shape[0], got_ref.shape[3]
    length = pieces * rows
    for slot in range(slots):
        code = got_ref[:, slot, planes].astype(jnp.int32).astype(F32).reshape(length, length)
        scales[slot] = decoded_scale(code)
    sums[...] = jnp.zeros_like(sums)
    for pair in range(planes // 2):
        totals = [[jnp.zeros((length, length), F32) for _ in range(bands)] for _ in range(2)]
        for slot, (which, first, second) in enumerate(table):
            lines = []
            for side in range(2):
                value = got_ref[:, slot, pair * 2 + side].astype(jnp.int32).astype(F32)
                lines.append(value.reshape(length, length) * scales[slot])
            lines = from_left(jnp.concatenate(lines, axis=1), left_ref[...])
            lines = jnp.concatenate([lines[:, :length], lines[:, length:]], axis=0)
            lines = from_right(lines, right_ref[...])
            for side in range(2):
                plane = pair * 2 + side
                term = lines[side * length : (side + 1) * length] * partner_plane(
                    resident_ref, received_ref, which, second, plane
                )
                for band in range(bands):
                    totals[side][band] += jnp.where(first == band, term, 0.0)
        for side in range(2):
            plane = pair * 2 + side
            for band in range(bands):
                out_ref[band, plane] = totals[side][band].astype(out_ref.dtype)
                for other in range(bands):
                    product = own_ref[other, plane].astype(F32) * totals[side][band]
                    sums[other * bands + band] += product.reshape(length // 8, 8, length).sum(axis=0)

    for entry in range(bands * bands):
        row = jnp.sum(sums[entry], axis=0, keepdims=True)
        terms_ref[:, entry // bands, entry % bands : entry % bands + 1, :] = jnp.broadcast_to(
            row[None], (terms_ref.shape[0], 1, row.shape[1])
        )


VMEM = pl.BlockSpec(memory_space=pltpu.VMEM)
SMEM = pl.BlockSpec(memory_space=pltpu.SMEM)
ANY = pl.BlockSpec(memory_space=pl.ANY)


def on_device(right, left, own_orbitals, resident_orbitals, pair_lists, pair_counts):
    bands, planes, length = own_orbitals.shape[:3]
    pieces = lax.axis_size("grid")
    rows = length // pieces
    received = passed_along(resident_orbitals, "band", 1)
    lists, counts = pair_lists, pair_counts
    field = pltpu.VMEM((planes, length, length), F32)

    def coded(slots):
        return jax.ShapeDtypeStruct((pieces, slots, planes + 1, rows, length), jnp.int16)

    early, kernel, index = pl.pallas_call(
        early_kernel,
        out_shape=(
            coded(2),
            jax.ShapeDtypeStruct((length, rows * length), F32),
            jax.ShapeDtypeStruct((1,), jnp.int32),
        ),
        in_specs=[SMEM, SMEM, ANY, ANY, VMEM, VMEM],
        out_specs=(VMEM, VMEM, SMEM),
        scratch_shapes=[
            field,
            pltpu.VMEM(own_orbitals.shape, BF16),
            pltpu.VMEM(own_orbitals.shape, BF16),
            pltpu.SemaphoreType.DMA((2,)),
        ],
        cost_estimate=pl.CostEstimate(
            flops=600_000_000, bytes_accessed=3_000_000, transcendentals=0
        ),
        compiler_params=LIMIT,
        name="early",
    )(lists, counts, own_orbitals, resident_orbitals, right, left)

    def branch(slots):
        def run(own_orbitals, resident_orbitals, received, lists, counts, early, kernel, right, left):
            sent = pl.pallas_call(
                functools.partial(late_kernel, slots),
                out_shape=coded(slots),
                in_specs=[SMEM, SMEM, VMEM, VMEM, VMEM, VMEM, VMEM],
                out_specs=VMEM,
                scratch_shapes=[field],
                compiler_params=LIMIT,
                name="late",
            )(lists, counts, own_orbitals, received, early, right, left)
            got = lax.all_to_all(sent, "grid", split_axis=0, concat_axis=0, tiled=True)
            sent = pl.pallas_call(
                functools.partial(middle_kernel, slots),
                out_shape=coded(slots),
                in_specs=[VMEM, VMEM, VMEM],
                out_specs=VMEM,
                scratch_shapes=[pltpu.VMEM((slots, length * rows, length), F32)] * 2,
                compiler_params=LIMIT,
                name="middle",
            )(got, kernel, left)
            got = lax.all_to_all(sent, "grid", split_axis=0, concat_axis=0, tiled=True)
            return pl.pallas_call(
                functools.partial(final_kernel, slots),
                out_shape=(
                    jax.ShapeDtypeStruct(own_orbitals.shape, BF16),
                    jax.ShapeDtypeStruct((pieces, bands, bands, length), F32),
                ),
                in_specs=[SMEM, SMEM, VMEM, VMEM, VMEM, VMEM, VMEM, VMEM],
                out_specs=(VMEM, VMEM),
                scratch_shapes=[
                    pltpu.VMEM((slots, length, length), F32),
                    pltpu.VMEM((bands * bands, 8, length), F32),
                ],
                compiler_params=LIMIT,
                name="final",
            )(lists, counts, own_orbitals, resident_orbitals, received, got, right, left)

        return run

    exchange, terms = lax.switch(
        index[0],
        [branch(2), branch(3), branch(4)],
        own_orbitals,
        resident_orbitals,
        received,
        lists,
        counts,
        early,
        kernel,
        right,
        left,
    )
    terms = lax.all_to_all(terms, "grid", split_axis=0, concat_axis=0, tiled=True)
    return exchange, jnp.sum(terms, axis=(0, 3))


def solution(mesh):
    in_specs = (
        P(None, None),
        P(None, None),
        P("band", "grid", None, None),
        P("band", "grid", None, None),
        P("band", None, None, None),
        P("band", None),
    )
    out_specs = (P("band", "grid", None, None), P("band", None))
    mapped = jax.shard_map(
        on_device, mesh=mesh, in_specs=in_specs, out_specs=out_specs, check_vma=False
    )

    def step(own_orbitals, resident_orbitals, pair_lists, pair_counts):
        length = own_orbitals.shape[-1]
        right, left = jnp.asarray(right_table(length)), jnp.asarray(left_table(length))
        return mapped(right, left, own_orbitals, resident_orbitals, pair_lists, pair_counts)

    return step
```

```python
import functools
import math

import jax
import jax.numpy as jnp
import numpy as np
from jax import lax
from jax.experimental import pallas as pl
from jax.experimental.pallas import tpu as pltpu
from jax.sharding import PartitionSpec as P

BF16 = jnp.bfloat16
F32 = jnp.float32
TOP = 32766.0
STEPS = 256.0
GROUP = 4
LIMIT = pltpu.CompilerParams(vmem_limit_bytes=20 << 20)


def passed_along(x, axis, by):
    length = lax.axis_size(axis)
    return lax.ppermute(x, axis, [(i, (i + by) % length) for i in range(length)])


def cas_halves(length):
    indices = np.arange(length)
    angles = (indices[:, None] * indices[None, :] % length) * (2.0 * math.pi / length)
    table = (np.cos(angles) + np.sin(angles)) / math.sqrt(length)
    high = table.astype(np.float32).astype(BF16)
    low = (table - high.astype(np.float64)).astype(np.float32).astype(BF16)
    return high, low


def right_table(length):
    high, low = cas_halves(length)
    row = np.concatenate([high, low], axis=1)
    return np.concatenate([row, row], axis=0)


def left_table(length):
    high, low = cas_halves(length)
    column = np.concatenate([high, low], axis=0)
    return np.concatenate([column, column], axis=1)


def halves(x):
    high = x.astype(BF16)
    return high, (x - high.astype(F32)).astype(BF16)


def from_right(x, table):
    half = x.shape[1]
    both = jnp.dot(jnp.concatenate(halves(x), axis=1), table, preferred_element_type=F32)
    return both[:, :half] + both[:, half:]


def from_left(x, table):
    half = x.shape[0]
    both = jnp.dot(table, jnp.concatenate(halves(x), axis=0), preferred_element_type=F32)
    return both[:half] + both[half:]


def scale_code(peak):
    return jnp.ceil(jnp.log2(jnp.maximum(peak, 1e-37)) * STEPS)


def decoded_scale(code):
    return jnp.exp2(code * (1.0 / STEPS)) * (1.0 / TOP)


def encode(load, store, planes, carry):
    values = [load(plane) for plane in range(planes)]
    peak = functools.reduce(jnp.maximum, [jnp.abs(value) for value in values])
    code = scale_code(peak)
    inverse = jnp.exp2(code * (-1.0 / STEPS)) * TOP
    left = None
    for plane, value in enumerate(values):
        scaled = value * inverse
        if left is not None:
            scaled = scaled + left
        whole = jnp.round(scaled)
        if carry:
            left = scaled - whole
        store(plane, whole.astype(jnp.int32))
    store(planes, code.astype(jnp.int32))


def store_coded(out_ref, piece, slot, rows):
    def store(plane, value):
        count = value.shape[0] // rows
        value = value.reshape(count, rows, value.shape[1]).astype(jnp.int16)
        out_ref[pl.ds(piece, count), slot, plane] = value

    return store


def forward_slot(own_ref, first, partner_ref, second, right_ref, left_ref, out_ref, slot, field):
    planes, length = own_ref.shape[1], own_ref.shape[2]
    pieces, rows = out_ref.shape[0], out_ref.shape[3]
    for pair in range(planes // 2):
        densities = [
            own_ref[first, plane].astype(F32) * partner_ref[second, plane].astype(F32)
            for plane in (pair * 2, pair * 2 + 1)
        ]
        lines = from_right(jnp.concatenate(densities, axis=0), right_ref[...])
        lines = jnp.concatenate([lines[:length], lines[length:]], axis=1)
        lines = from_left(lines, left_ref[...])
        for side in range(2):
            field[pair * 2 + side] = lines[:, side * length : (side + 1) * length]
    for piece in range(0, pieces, GROUP):
        encode(
            lambda plane: field[plane, pl.ds(piece * rows, GROUP * rows), :],
            store_coded(out_ref, piece, slot, rows),
            planes,
            True,
        )


def early_kernel(
    lists_ref,
    counts_ref,
    own_hbm,
    resident_hbm,
    right_ref,
    left_ref,
    out_ref,
    kernel_ref,
    index_ref,
    field,
    own_ref,
    resident_ref,
    sems,
):
    slots, rows, length = out_ref.shape[1], out_ref.shape[3], out_ref.shape[4]
    copies = []
    for number, (source, target) in enumerate(((own_hbm, own_ref), (resident_hbm, resident_ref))):
        copy = pltpu.make_async_copy(source, target, sems.at[number])
        copy.start()
        copies.append(copy)
    index_ref[0] = counts_ref[0, 0] + counts_ref[0, 1] - 2
    place = lax.axis_index("grid")
    first = lax.broadcasted_iota(jnp.int32, (length, length), 0)
    last = lax.broadcasted_iota(jnp.int32, (length, length), 1)
    first = jnp.minimum(first, length - first).astype(F32)
    last = jnp.minimum(last, length - last).astype(F32)
    around = first * first + last * last
    for row in range(rows):
        middle = place * rows + row
        middle = jnp.minimum(middle, length - middle).astype(F32)
        squared = around + middle * middle
        kernel_ref[:, row * length : (row + 1) * length] = jnp.where(
            squared > 0.5, 0.25 * length**1.5 / jnp.maximum(squared, 1.0), 0.0
        )
    for copy in copies:
        copy.wait()

    def transform(slot):
        forward_slot(
            own_ref,
            lists_ref[0, 0, slot, 0],
            resident_ref,
            lists_ref[0, 0, slot, 1],
            right_ref,
            left_ref,
            out_ref,
            slot,
            field,
        )

    transform(0)
    for slot in range(1, slots):

        @pl.when(slot < counts_ref[0, 0])
        def _():
            transform(slot)


def late_kernel(
    slots, lists_ref, counts_ref, own_ref, received_ref, early_ref, right_ref, left_ref, out_ref, field
):
    def transform(number, slot):
        forward_slot(
            own_ref,
            lists_ref[0, 1, number, 0],
            received_ref,
            lists_ref[0, 1, number, 1],
            right_ref,
            left_ref,
            out_ref,
            slot,
            field,
        )

    out_ref[:, 0] = early_ref[:, 0]
    transform(0, 1)
    if slots == 3:

        @pl.when(counts_ref[0, 0] == 2)
        def _():
            out_ref[:, 2] = early_ref[:, 1]

        @pl.when(counts_ref[0, 0] != 2)
        def _():
            transform(1, 2)

    if slots == 4:
        out_ref[:, 2] = early_ref[:, 1]
        transform(1, 3)


def middle_kernel(slots, got_ref, kernel_ref, left_ref, out_ref, before, after):
    pieces, rows = got_ref.shape[0], got_ref.shape[3]
    planes = got_ref.shape[2] - 1
    length = pieces * planes
    for slot in range(slots):
        for piece in range(pieces):
            scale = decoded_scale(got_ref[piece, slot, planes].astype(jnp.int32).astype(F32))
            for plane in range(planes):
                start = (piece * planes + plane) * rows
                before[slot, pl.ds(start, rows), :] = (
                    got_ref[piece, slot, plane].astype(jnp.int32).astype(F32) * scale
                )
        for pair in range(rows // 2):
            lines = jnp.concatenate(
                [before[slot, pl.ds(pair * 2 + side, length, stride=rows), :] for side in range(2)],
                axis=1,
            )
            lines = from_left(lines, left_ref[...])
            lines = lines * kernel_ref[:, pair * 2 * length : (pair + 1) * 2 * length]
            lines = from_left(lines, left_ref[...])
            for side in range(2):
                after[slot, pl.ds(pair * 2 + side, length, stride=rows), :] = lines[
                    :, side * length : (side + 1) * length
                ]
        for piece in range(pieces):
            encode(
                lambda plane: after[slot, pl.ds((piece * planes + plane) * rows, rows), :],
                store_coded(out_ref, piece, slot, rows),
                planes,
                False,
            )


def slot_table(lists_ref, counts_ref, slots):
    table = []
    for slot in range(slots):
        if slot < 2:
            which, place = slot, 0
        elif slots == 3:
            which, place = jnp.where(counts_ref[0, 0] == 2, 0, 1), 1
        else:
            which, place = slot - 2, 1
        table.append((which, lists_ref[0, which, place, 0], lists_ref[0, which, place, 1]))
    return table


def partner_plane(resident_ref, received_ref, which, band, plane):
    if isinstance(which, int):
        chosen = received_ref if which else resident_ref
        return chosen[band, plane].astype(F32)
    return jnp.where(
        which == 1, received_ref[band, plane].astype(F32), resident_ref[band, plane].astype(F32)
    )


def cross_kernel(
    slots, lists_ref, counts_ref, own_ref, resident_ref, received_ref, right_ref, left_ref, out_ref
):
    bands, planes, length = own_ref.shape[:3]
    for slot, (which, _, second) in enumerate(slot_table(lists_ref, counts_ref, slots)):
        for plane in range(planes):
            partner = partner_plane(resident_ref, received_ref, which, second, plane)
            densities = [own_ref[band, plane].astype(F32) * partner for band in range(bands)]
            lines = from_right(jnp.concatenate(densities, axis=0), right_ref[...])
            lines = jnp.concatenate([lines[:length], lines[length:]], axis=1)
            lines = from_left(lines, left_ref[...])
            for band in range(bands):
                out_ref[slot, band, plane] = lines[:, band * length : (band + 1) * length]


def inner_kernel(slots, lists_ref, counts_ref, got_ref, spectra_ref, terms_ref):
    bands, planes, length = spectra_ref.shape[1:4]
    sums = [[jnp.zeros((8, length), F32) for _ in range(bands)] for _ in range(bands)]
    for slot, (_, first, _) in enumerate(slot_table(lists_ref, counts_ref, slots)):
        code = got_ref[:, slot, planes].astype(jnp.int32).astype(F32).reshape(length, length)
        scale = decoded_scale(code)
        totals = [jnp.zeros((length, length), F32) for _ in range(bands)]
        for plane in range(planes):
            value = got_ref[:, slot, plane].astype(jnp.int32).astype(F32).reshape(length, length)
            for band in range(bands):
                totals[band] += value * spectra_ref[slot, band, plane]
        for band in range(bands):
            total = (totals[band] * scale).reshape(length // 8, 8, length).sum(axis=0)
            for other in range(bands):
                sums[band][other] += jnp.where(first == other, total, 0.0)
    for band in range(bands):
        for other in range(bands):
            row = jnp.sum(sums[band][other], axis=0, keepdims=True)
            terms_ref[:, band, other : other + 1, :] = jnp.broadcast_to(
                row[None], (terms_ref.shape[0], 1, length)
            )


def final_kernel(
    slots,
    lists_ref,
    counts_ref,
    resident_ref,
    received_ref,
    got_ref,
    right_ref,
    left_ref,
    out_ref,
    scales,
):
    table = slot_table(lists_ref, counts_ref, slots)
    bands, planes, length = out_ref.shape[:3]
    for slot in range(slots):
        code = got_ref[:, slot, planes].astype(jnp.int32).astype(F32).reshape(length, length)
        scales[slot] = decoded_scale(code)
    for pair in range(planes // 2):
        totals = [[jnp.zeros((length, length), F32) for _ in range(bands)] for _ in range(2)]
        for slot, (which, first, second) in enumerate(table):
            lines = []
            for side in range(2):
                value = got_ref[:, slot, pair * 2 + side].astype(jnp.int32).astype(F32)
                lines.append(value.reshape(length, length) * scales[slot])
            lines = from_left(jnp.concatenate(lines, axis=1), left_ref[...])
            lines = jnp.concatenate([lines[:, :length], lines[:, length:]], axis=0)
            lines = from_right(lines, right_ref[...])
            for side in range(2):
                plane = pair * 2 + side
                term = lines[side * length : (side + 1) * length] * partner_plane(
                    resident_ref, received_ref, which, second, plane
                )
                for band in range(bands):
                    totals[side][band] += jnp.where(first == band, term, 0.0)
        for side in range(2):
            for band in range(bands):
                out_ref[band, pair * 2 + side] = totals[side][band].astype(out_ref.dtype)


VMEM = pl.BlockSpec(memory_space=pltpu.VMEM)
SMEM = pl.BlockSpec(memory_space=pltpu.SMEM)
ANY = pl.BlockSpec(memory_space=pl.ANY)


def on_device(right, left, own_orbitals, resident_orbitals, pair_lists, pair_counts):
    bands, planes, length = own_orbitals.shape[:3]
    pieces = lax.axis_size("grid")
    rows = length // pieces
    received = passed_along(resident_orbitals, "band", 1)
    lists, counts = pair_lists, pair_counts
    field = pltpu.VMEM((planes, length, length), F32)

    def coded(slots):
        return jax.ShapeDtypeStruct((pieces, slots, planes + 1, rows, length), jnp.int16)

    early, kernel, index = pl.pallas_call(
        early_kernel,
        out_shape=(
            coded(2),
            jax.ShapeDtypeStruct((length, rows * length), F32),
            jax.ShapeDtypeStruct((1,), jnp.int32),
        ),
        in_specs=[SMEM, SMEM, ANY, ANY, VMEM, VMEM],
        out_specs=(VMEM, VMEM, SMEM),
        scratch_shapes=[
            field,
            pltpu.VMEM(own_orbitals.shape, BF16),
            pltpu.VMEM(own_orbitals.shape, BF16),
            pltpu.SemaphoreType.DMA((2,)),
        ],
        cost_estimate=pl.CostEstimate(
            flops=600_000_000, bytes_accessed=3_000_000, transcendentals=0
        ),
        compiler_params=LIMIT,
        name="early",
    )(lists, counts, own_orbitals, resident_orbitals, right, left)

    def branch(slots):
        def run(own_orbitals, resident_orbitals, received, lists, counts, early, kernel, right, left):
            sent = pl.pallas_call(
                functools.partial(late_kernel, slots),
                out_shape=coded(slots),
                in_specs=[SMEM, SMEM, VMEM, VMEM, VMEM, VMEM, VMEM],
                out_specs=VMEM,
                scratch_shapes=[field],
                compiler_params=LIMIT,
                name="late",
            )(lists, counts, own_orbitals, received, early, right, left)
            got = lax.all_to_all(sent, "grid", split_axis=0, concat_axis=0, tiled=True)
            spectra = pl.pallas_call(
                functools.partial(cross_kernel, slots),
                out_shape=jax.ShapeDtypeStruct((slots, bands, planes, length, length), F32),
                in_specs=[SMEM, SMEM, VMEM, VMEM, VMEM, VMEM, VMEM],
                out_specs=VMEM,
                cost_estimate=pl.CostEstimate(
                    flops=400_000_000 * slots, bytes_accessed=1_500_000, transcendentals=0
                ),
                compiler_params=LIMIT,
                name="cross",
            )(lists, counts, own_orbitals, resident_orbitals, received, right, left)
            sent = pl.pallas_call(
                functools.partial(middle_kernel, slots),
                out_shape=coded(slots),
                in_specs=[VMEM, VMEM, VMEM],
                out_specs=VMEM,
                scratch_shapes=[pltpu.VMEM((slots, length * rows, length), F32)] * 2,
                compiler_params=LIMIT,
                name="middle",
            )(got, kernel, left)
            got = lax.all_to_all(sent, "grid", split_axis=0, concat_axis=0, tiled=True)
            terms = pl.pallas_call(
                functools.partial(inner_kernel, slots),
                out_shape=jax.ShapeDtypeStruct((pieces, bands, bands, length), F32),
                in_specs=[SMEM, SMEM, VMEM, VMEM],
                out_specs=VMEM,
                compiler_params=LIMIT,
                name="inner",
            )(lists, counts, got, spectra)
            terms = lax.all_to_all(terms, "grid", split_axis=0, concat_axis=0, tiled=True)
            exchange = pl.pallas_call(
                functools.partial(final_kernel, slots),
                out_shape=jax.ShapeDtypeStruct(own_orbitals.shape, BF16),
                in_specs=[SMEM, SMEM, VMEM, VMEM, VMEM, VMEM, VMEM],
                out_specs=VMEM,
                scratch_shapes=[pltpu.VMEM((slots, length, length), F32)],
                cost_estimate=pl.CostEstimate(
                    flops=400_000_000 * slots, bytes_accessed=2_000_000, transcendentals=0
                ),
                compiler_params=LIMIT,
                name="final",
            )(lists, counts, resident_orbitals, received, got, right, left)
            return exchange, jnp.sum(terms, axis=(0, 3))

        return run

    return lax.switch(
        index[0],
        [branch(2), branch(3), branch(4)],
        own_orbitals,
        resident_orbitals,
        received,
        lists,
        counts,
        early,
        kernel,
        right,
        left,
    )


def solution(mesh):
    in_specs = (
        P(None, None),
        P(None, None),
        P("band", "grid", None, None),
        P("band", "grid", None, None),
        P("band", None, None, None),
        P("band", None),
    )
    out_specs = (P("band", "grid", None, None), P("band", None))
    mapped = jax.shard_map(
        on_device, mesh=mesh, in_specs=in_specs, out_specs=out_specs, check_vma=False
    )

    def step(own_orbitals, resident_orbitals, pair_lists, pair_counts):
        length = own_orbitals.shape[-1]
        right, left = jnp.asarray(right_table(length)), jnp.asarray(left_table(length))
        return mapped(right, left, own_orbitals, resident_orbitals, pair_lists, pair_counts)

    return step
```

```python
import functools
import math

import jax
import jax.numpy as jnp
import numpy as np
from jax import lax
from jax.experimental import pallas as pl
from jax.experimental.pallas import tpu as pltpu
from jax.sharding import PartitionSpec as P

BF16 = jnp.bfloat16
F32 = jnp.float32
TOP = 32766.0
STEPS = 256.0
GROUP = 4
OUT_SHARE = 4
BACK_SHARE = 2
LIMIT = pltpu.CompilerParams(vmem_limit_bytes=20 << 20)


def passed_along(x, axis, by):
    length = lax.axis_size(axis)
    return lax.ppermute(x, axis, [(i, (i + by) % length) for i in range(length)])


def cas_halves(length):
    indices = np.arange(length)
    angles = (indices[:, None] * indices[None, :] % length) * (2.0 * math.pi / length)
    table = (np.cos(angles) + np.sin(angles)) / math.sqrt(length)
    high = table.astype(np.float32).astype(BF16)
    low = (table - high.astype(np.float64)).astype(np.float32).astype(BF16)
    return high, low


def right_table(length):
    high, low = cas_halves(length)
    row = np.concatenate([high, low], axis=1)
    return np.concatenate([row, row], axis=0)


def left_table(length):
    high, low = cas_halves(length)
    column = np.concatenate([high, low], axis=0)
    return np.concatenate([column, column], axis=1)


def halves(x):
    high = x.astype(BF16)
    return high, (x - high.astype(F32)).astype(BF16)


def from_right(x, table):
    half = x.shape[1]
    both = jnp.dot(jnp.concatenate(halves(x), axis=1), table, preferred_element_type=F32)
    return both[:, :half] + both[:, half:]


def from_left(x, table):
    half = x.shape[0]
    both = jnp.dot(table, jnp.concatenate(halves(x), axis=0), preferred_element_type=F32)
    return both[:half] + both[half:]


def scale_code(peak):
    return jnp.ceil(jnp.log2(jnp.maximum(peak, 1e-37)) * STEPS)


def decoded_scale(code):
    return jnp.exp2(code * (1.0 / STEPS)) * (1.0 / TOP)


def lane_group(shape, share):
    return lax.broadcasted_iota(jnp.int32, shape, 1) // (shape[1] // share)


def over_lanes(x, share, combine):
    step = x.shape[1]
    while share > 1:
        step, share = step // 2, share // 2
        x = combine(x, pltpu.roll(x, step, 1))
    return x


def packed_codes(codes, share):
    tiles = []
    for start in range(0, len(codes), share):
        tile = codes[start]
        group = lane_group(tile.shape, share)
        for offset, code in enumerate(codes[start + 1 : start + share]):
            tile = jnp.where(group == offset + 1, code, tile)
        tiles.append(tile)
    return tiles


def unpacked_scale(tile, place, share):
    group = lane_group(tile.shape, share)
    return decoded_scale(over_lanes(jnp.where(group == place, tile, 0.0), share, jnp.add))


def encode(load, store, planes, carry, share):
    values = [load(plane) for plane in range(planes)]
    peak = functools.reduce(jnp.maximum, [jnp.abs(value) for value in values])
    code = scale_code(over_lanes(peak, share, jnp.maximum))
    inverse = jnp.exp2(code * (-1.0 / STEPS)) * TOP
    left = None
    for plane, value in enumerate(values):
        scaled = value * inverse
        if left is not None:
            scaled = scaled + left
        whole = jnp.round(scaled)
        if carry:
            left = scaled - whole
        store(plane, whole.astype(jnp.int32))
    return code


def store_coded(out_ref, piece, first):
    rows = out_ref.shape[2]

    def store(plane, value):
        count = value.shape[0] // rows
        value = value.reshape(count, rows, value.shape[1]).astype(jnp.int16)
        out_ref[pl.ds(piece, count), first + plane] = value

    return store


def store_tile(out_ref, number, tile):
    pieces, _, rows, length = out_ref.shape
    out_ref[:, number] = tile.astype(jnp.int32).reshape(pieces, rows, length).astype(jnp.int16)


def load_tile(got_ref, number):
    pieces, _, rows, length = got_ref.shape
    return got_ref[:, number].astype(jnp.int32).astype(F32).reshape(pieces * rows, length)


def forward_slot(own_ref, first, partner_ref, second, right_ref, left_ref, out_ref, start, field, code_ref):
    planes, length = own_ref.shape[1], own_ref.shape[2]
    pieces, rows = out_ref.shape[0], out_ref.shape[2]
    for pair in range(planes // 2):
        densities = [
            own_ref[first, plane].astype(F32) * partner_ref[second, plane].astype(F32)
            for plane in (pair * 2, pair * 2 + 1)
        ]
        lines = from_right(jnp.concatenate(densities, axis=0), right_ref[...])
        lines = jnp.concatenate([lines[:length], lines[length:]], axis=1)
        lines = from_left(lines, left_ref[...])
        for side in range(2):
            field[pair * 2 + side] = lines[:, side * length : (side + 1) * length]
    for piece in range(0, pieces, GROUP):
        code_ref[pl.ds(piece * rows, GROUP * rows), :] = encode(
            lambda plane: field[plane, pl.ds(piece * rows, GROUP * rows), :],
            store_coded(out_ref, piece, start),
            planes,
            True,
            OUT_SHARE,
        )


def early_kernel(
    lists_ref,
    counts_ref,
    own_hbm,
    resident_hbm,
    right_ref,
    left_ref,
    out_ref,
    kernel_ref,
    codes_ref,
    index_ref,
    field,
    own_ref,
    resident_ref,
    sems,
):
    rows, length = out_ref.shape[2], out_ref.shape[3]
    slots, planes = codes_ref.shape[0], own_ref.shape[1]
    copies = []
    for number, (source, target) in enumerate(((own_hbm, own_ref), (resident_hbm, resident_ref))):
        copy = pltpu.make_async_copy(source, target, sems.at[number])
        copy.start()
        copies.append(copy)
    index_ref[0] = counts_ref[0, 0] + counts_ref[0, 1] - 2
    place = lax.axis_index("grid")
    first = lax.broadcasted_iota(jnp.int32, (length, length), 0)
    last = lax.broadcasted_iota(jnp.int32, (length, length), 1)
    first = jnp.minimum(first, length - first).astype(F32)
    last = jnp.minimum(last, length - last).astype(F32)
    around = first * first + last * last
    for row in range(rows):
        middle = place * rows + row
        middle = jnp.minimum(middle, length - middle).astype(F32)
        squared = around + middle * middle
        kernel_ref[:, row * length : (row + 1) * length] = jnp.where(
            squared > 0.5, 0.25 * length**1.5 / jnp.maximum(squared, 1.0), 0.0
        )
    for copy in copies:
        copy.wait()

    def transform(slot):
        forward_slot(
            own_ref,
            lists_ref[0, 0, slot, 0],
            resident_ref,
            lists_ref[0, 0, slot, 1],
            right_ref,
            left_ref,
            out_ref,
            slot * planes,
            field,
            codes_ref.at[slot],
        )

    transform(0)
    for slot in range(1, slots):

        @pl.when(slot < counts_ref[0, 0])
        def _():
            transform(slot)


def late_kernel(
    slots,
    lists_ref,
    counts_ref,
    own_ref,
    received_ref,
    early_ref,
    early_codes_ref,
    right_ref,
    left_ref,
    out_ref,
    field,
    codes,
):
    planes = own_ref.shape[1]

    def transform(number, slot):
        forward_slot(
            own_ref,
            lists_ref[0, 1, number, 0],
            received_ref,
            lists_ref[0, 1, number, 1],
            right_ref,
            left_ref,
            out_ref,
            slot * planes,
            field,
            codes.at[slot],
        )

    def take(number, slot):
        out_ref[:, slot * planes : (slot + 1) * planes] = early_ref[
            :, number * planes : (number + 1) * planes
        ]
        codes[slot] = early_codes_ref[number]

    take(0, 0)
    transform(0, 1)
    if slots == 3:

        @pl.when(counts_ref[0, 0] == 2)
        def _():
            take(1, 2)

        @pl.when(counts_ref[0, 0] != 2)
        def _():
            transform(1, 2)

    if slots == 4:
        take(1, 2)
        transform(1, 3)
    for number, tile in enumerate(packed_codes([codes[slot] for slot in range(slots)], OUT_SHARE)):
        store_tile(out_ref, slots * planes + number, tile)


def middle_kernel(slots, planes, got_ref, kernel_ref, left_ref, out_ref, before, after, codes):
    pieces, rows = got_ref.shape[0], got_ref.shape[2]
    length = pieces * planes
    for slot in range(slots):
        tile = load_tile(got_ref, slots * planes + slot // OUT_SHARE)
        codes[slot] = unpacked_scale(tile, slot % OUT_SHARE, OUT_SHARE)
    for slot in range(slots):
        for piece in range(pieces):
            scale = codes[slot, pl.ds(piece * rows, rows), :]
            for plane in range(planes):
                start = (piece * planes + plane) * rows
                before[slot, pl.ds(start, rows), :] = (
                    got_ref[piece, slot * planes + plane].astype(jnp.int32).astype(F32) * scale
                )
        for pair in range(rows // 2):
            lines = jnp.concatenate(
                [before[slot, pl.ds(pair * 2 + side, length, stride=rows), :] for side in range(2)],
                axis=1,
            )
            lines = from_left(lines, left_ref[...])
            lines = lines * kernel_ref[:, pair * 2 * length : (pair + 1) * 2 * length]
            lines = from_left(lines, left_ref[...])
            for side in range(2):
                after[slot, pl.ds(pair * 2 + side, length, stride=rows), :] = lines[
                    :, side * length : (side + 1) * length
                ]
        for piece in range(pieces):
            codes[slot, pl.ds(piece * rows, rows), :] = encode(
                lambda plane: after[slot, pl.ds((piece * planes + plane) * rows, rows), :],
                store_coded(out_ref, piece, slot * planes),
                planes,
                False,
                BACK_SHARE,
            )
    for number, tile in enumerate(packed_codes([codes[slot] for slot in range(slots)], BACK_SHARE)):
        store_tile(out_ref, slots * planes + number, tile)


def slot_table(lists_ref, counts_ref, slots):
    table = []
    for slot in range(slots):
        if slot < 2:
            which, place = slot, 0
        elif slots == 3:
            which, place = jnp.where(counts_ref[0, 0] == 2, 0, 1), 1
        else:
            which, place = slot - 2, 1
        table.append((which, lists_ref[0, which, place, 0], lists_ref[0, which, place, 1]))
    return table


def partner_plane(resident_ref, received_ref, which, band, plane):
    if isinstance(which, int):
        chosen = received_ref if which else resident_ref
        return chosen[band, plane].astype(F32)
    return jnp.where(
        which == 1, received_ref[band, plane].astype(F32), resident_ref[band, plane].astype(F32)
    )


def final_kernel(
    slots,
    lists_ref,
    counts_ref,
    own_ref,
    resident_ref,
    received_ref,
    got_ref,
    right_ref,
    left_ref,
    out_hbm,
    terms_ref,
    scales,
    sums,
    out_ref,
    sems,
):
    table = slot_table(lists_ref, counts_ref, slots)
    bands, planes, length = own_ref.shape[:3]
    for slot in range(slots):
        tile = load_tile(got_ref, slots * planes + slot // BACK_SHARE)
        scales[slot] = unpacked_scale(tile, slot % BACK_SHARE, BACK_SHARE)
    sums[...] = jnp.zeros_like(sums)

    def copies(pair):
        return [
            pltpu.make_async_copy(
                out_ref.at[band, pl.ds(pair * 2, 2)],
                out_hbm.at[band, pl.ds(pair * 2, 2)],
                sems.at[pair, band],
            )
            for band in range(bands)
        ]

    for pair in range(planes // 2):
        totals = [[jnp.zeros((length, length), F32) for _ in range(bands)] for _ in range(2)]
        for slot, (which, first, second) in enumerate(table):
            lines = []
            for side in range(2):
                value = load_tile(got_ref, slot * planes + pair * 2 + side)
                lines.append(value * scales[slot])
            lines = from_left(jnp.concatenate(lines, axis=1), left_ref[...])
            lines = jnp.concatenate([lines[:, :length], lines[:, length:]], axis=0)
            lines = from_right(lines, right_ref[...])
            for side in range(2):
                plane = pair * 2 + side
                term = lines[side * length : (side + 1) * length] * partner_plane(
                    resident_ref, received_ref, which, second, plane
                )
                for band in range(bands):
                    totals[side][band] += jnp.where(first == band, term, 0.0)
        for side in range(2):
            plane = pair * 2 + side
            for band in range(bands):
                out_ref[band, plane] = totals[side][band].astype(out_ref.dtype)
                for other in range(bands):
                    product = own_ref[other, plane].astype(F32) * totals[side][band]
                    sums[other * bands + band] += product.reshape(length // 8, 8, length).sum(axis=0)
        if pair:
            for copy in copies(pair - 1):
                copy.start()

    for entry in range(bands * bands):
        row = jnp.sum(sums[entry], axis=0, keepdims=True)
        terms_ref[:, entry // bands, entry % bands : entry % bands + 1, :] = jnp.broadcast_to(
            row[None], (terms_ref.shape[0], 1, row.shape[1])
        )
    for copy in copies(planes // 2 - 1):
        copy.start()
    for pair in range(planes // 2):
        for copy in copies(pair):
            copy.wait()


VMEM = pl.BlockSpec(memory_space=pltpu.VMEM)
SMEM = pl.BlockSpec(memory_space=pltpu.SMEM)
ANY = pl.BlockSpec(memory_space=pl.ANY)


def on_device(right, left, own_orbitals, resident_orbitals, pair_lists, pair_counts):
    bands, planes, length = own_orbitals.shape[:3]
    pieces = lax.axis_size("grid")
    rows = length // pieces
    received = passed_along(resident_orbitals, "band", 1)
    lists, counts = pair_lists, pair_counts
    field = pltpu.VMEM((planes, length, length), F32)

    table = pltpu.VMEM((4, length, length), F32)

    def coded(slots, share):
        tiles = slots * planes + (-(-slots // share) if share else 0)
        return jax.ShapeDtypeStruct((pieces, tiles, rows, length), jnp.int16)

    early, kernel, codes, index = pl.pallas_call(
        early_kernel,
        out_shape=(
            coded(2, 0),
            jax.ShapeDtypeStruct((length, rows * length), F32),
            jax.ShapeDtypeStruct((2, length, length), F32),
            jax.ShapeDtypeStruct((1,), jnp.int32),
        ),
        in_specs=[SMEM, SMEM, ANY, ANY, VMEM, VMEM],
        out_specs=(VMEM, VMEM, VMEM, SMEM),
        scratch_shapes=[
            field,
            pltpu.VMEM(own_orbitals.shape, BF16),
            pltpu.VMEM(own_orbitals.shape, BF16),
            pltpu.SemaphoreType.DMA((2,)),
        ],
        cost_estimate=pl.CostEstimate(
            flops=600_000_000, bytes_accessed=3_000_000, transcendentals=0
        ),
        compiler_params=LIMIT,
        name="early",
    )(lists, counts, own_orbitals, resident_orbitals, right, left)

    def branch(slots):
        def run(own_orbitals, resident_orbitals, received, lists, counts, early, kernel, codes, right, left):
            sent = pl.pallas_call(
                functools.partial(late_kernel, slots),
                out_shape=coded(slots, OUT_SHARE),
                in_specs=[SMEM, SMEM, VMEM, VMEM, VMEM, VMEM, VMEM, VMEM],
                out_specs=VMEM,
                scratch_shapes=[field, table],
                compiler_params=LIMIT,
                name="late",
            )(lists, counts, own_orbitals, received, early, codes, right, left)
            got = lax.all_to_all(sent, "grid", split_axis=0, concat_axis=0, tiled=True)
            sent = pl.pallas_call(
                functools.partial(middle_kernel, slots, planes),
                out_shape=coded(slots, BACK_SHARE),
                in_specs=[VMEM, VMEM, VMEM],
                out_specs=VMEM,
                scratch_shapes=[pltpu.VMEM((slots, length * rows, length), F32)] * 2 + [table],
                compiler_params=LIMIT,
                name="middle",
            )(got, kernel, left)
            got = lax.all_to_all(sent, "grid", split_axis=0, concat_axis=0, tiled=True)
            return pl.pallas_call(
                functools.partial(final_kernel, slots),
                out_shape=(
                    jax.ShapeDtypeStruct(own_orbitals.shape, BF16),
                    jax.ShapeDtypeStruct((pieces, bands, bands, length), F32),
                ),
                in_specs=[SMEM, SMEM, VMEM, VMEM, VMEM, VMEM, VMEM, VMEM],
                out_specs=(ANY, VMEM),
                scratch_shapes=[
                    pltpu.VMEM((slots, length, length), F32),
                    pltpu.VMEM((bands * bands, 8, length), F32),
                    pltpu.VMEM(own_orbitals.shape, BF16),
                    pltpu.SemaphoreType.DMA((planes // 2, bands)),
                ],
                compiler_params=LIMIT,
                name="final",
            )(lists, counts, own_orbitals, resident_orbitals, received, got, right, left)

        return run

    exchange, terms = lax.switch(
        index[0],
        [branch(2), branch(3), branch(4)],
        own_orbitals,
        resident_orbitals,
        received,
        lists,
        counts,
        early,
        kernel,
        codes,
        right,
        left,
    )
    terms = lax.all_to_all(terms, "grid", split_axis=0, concat_axis=0, tiled=True)
    return exchange, jnp.sum(terms, axis=(0, 3))


def solution(mesh):
    in_specs = (
        P(None, None),
        P(None, None),
        P("band", "grid", None, None),
        P("band", "grid", None, None),
        P("band", None, None, None),
        P("band", None),
    )
    out_specs = (P("band", "grid", None, None), P("band", None))
    mapped = jax.shard_map(
        on_device, mesh=mesh, in_specs=in_specs, out_specs=out_specs, check_vma=False
    )

    def step(own_orbitals, resident_orbitals, pair_lists, pair_counts):
        length = own_orbitals.shape[-1]
        right, left = jnp.asarray(right_table(length)), jnp.asarray(left_table(length))
        return mapped(right, left, own_orbitals, resident_orbitals, pair_lists, pair_counts)

    return step
```

```python
import functools
import math

import jax
import jax.numpy as jnp
import numpy as np
from jax import lax
from jax.experimental import pallas as pl
from jax.experimental.pallas import tpu as pltpu
from jax.sharding import PartitionSpec as P

BF16 = jnp.bfloat16
F32 = jnp.float32
TOP = 32760.0
STEPS = 256.0
FLOOR = 2.0**-110
GROUP = 4
OUT_SHARE = 4
BACK_SHARE = 2
LIMIT = pltpu.CompilerParams(vmem_limit_bytes=20 << 20)


def passed_along(x, axis, by):
    length = lax.axis_size(axis)
    return lax.ppermute(x, axis, [(i, (i + by) % length) for i in range(length)])


def cas_halves(length):
    indices = np.arange(length)
    angles = (indices[:, None] * indices[None, :] % length) * (2.0 * math.pi / length)
    table = (np.cos(angles) + np.sin(angles)) / math.sqrt(length)
    high = table.astype(np.float32).astype(BF16)
    low = (table - high.astype(np.float64)).astype(np.float32).astype(BF16)
    return high, low


def right_table(length):
    high, low = cas_halves(length)
    row = np.concatenate([high, low], axis=1)
    return np.concatenate([row, row], axis=0)


def left_table(length):
    high, low = cas_halves(length)
    column = np.concatenate([high, low], axis=0)
    return np.concatenate([column, column], axis=1)


def halves(x):
    high = x.astype(BF16)
    return high, (x - high.astype(F32)).astype(BF16)


def from_right(x, table):
    half = x.shape[1]
    both = jnp.dot(jnp.concatenate(halves(x), axis=1), table, preferred_element_type=F32)
    return both[:, :half] + both[:, half:]


def from_left(x, table):
    half = x.shape[0]
    both = jnp.dot(table, jnp.concatenate(halves(x), axis=0), preferred_element_type=F32)
    return both[:half] + both[half:]


def scale_code(peak):
    return jnp.ceil(jnp.log2(jnp.maximum(peak, FLOOR)) * STEPS)


def decoded_scale(code):
    return jnp.exp2(code * (1.0 / STEPS)) * (1.0 / TOP)


def lane_group(shape, share):
    return lax.broadcasted_iota(jnp.int32, shape, 1) // (shape[1] // share)


def over_lanes(x, share, combine):
    step = x.shape[1]
    while share > 1:
        step, share = step // 2, share // 2
        x = combine(x, pltpu.roll(x, step, 1))
    return x


def packed_codes(codes, share):
    tiles = []
    for start in range(0, len(codes), share):
        tile = codes[start]
        group = lane_group(tile.shape, share)
        for offset, code in enumerate(codes[start + 1 : start + share]):
            tile = jnp.where(group == offset + 1, code, tile)
        tiles.append(tile)
    return tiles


def unpacked_scale(tile, place, share):
    group = lane_group(tile.shape, share)
    return decoded_scale(over_lanes(jnp.where(group == place, tile, 0.0), share, jnp.add))


def encode(load, store, planes, carry, share):
    values = [load(plane) for plane in range(planes)]
    peak = functools.reduce(jnp.maximum, [jnp.abs(value) for value in values])
    code = scale_code(over_lanes(peak, share, jnp.maximum))
    inverse = jnp.exp2(code * (-1.0 / STEPS)) * TOP
    left = None
    for plane, value in enumerate(values):
        scaled = value * inverse
        if left is not None:
            scaled = scaled + left
        whole = jnp.round(scaled)
        if carry:
            left = scaled - whole
        store(plane, whole.astype(jnp.int32))
    return code


def store_coded(out_ref, piece, first):
    rows = out_ref.shape[2]

    def store(plane, value):
        count = value.shape[0] // rows
        value = value.reshape(count, rows, value.shape[1]).astype(jnp.int16)
        out_ref[pl.ds(piece, count), first + plane] = value

    return store


def store_tile(out_ref, number, tile):
    pieces, _, rows, length = out_ref.shape
    out_ref[:, number] = tile.astype(jnp.int32).reshape(pieces, rows, length).astype(jnp.int16)


def load_tile(got_ref, number):
    pieces, _, rows, length = got_ref.shape
    return got_ref[:, number].astype(jnp.int32).astype(F32).reshape(pieces * rows, length)


def forward_slot(own_ref, first, partner_ref, second, right_ref, left_ref, out_ref, start, field, code_ref):
    planes, length = own_ref.shape[1], own_ref.shape[2]
    pieces, rows = out_ref.shape[0], out_ref.shape[2]
    for pair in range(planes // 2):
        densities = [
            own_ref[first, plane].astype(F32) * partner_ref[second, plane].astype(F32)
            for plane in (pair * 2, pair * 2 + 1)
        ]
        lines = from_right(jnp.concatenate(densities, axis=0), right_ref[...])
        lines = jnp.concatenate([lines[:length], lines[length:]], axis=1)
        lines = from_left(lines, left_ref[...])
        for side in range(2):
            field[pair * 2 + side] = lines[:, side * length : (side + 1) * length]
    for piece in range(0, pieces, GROUP):
        code_ref[pl.ds(piece * rows, GROUP * rows), :] = encode(
            lambda plane: field[plane, pl.ds(piece * rows, GROUP * rows), :],
            store_coded(out_ref, piece, start),
            planes,
            True,
            OUT_SHARE,
        )


def early_kernel(
    lists_ref,
    counts_ref,
    own_hbm,
    resident_hbm,
    right_ref,
    left_ref,
    out_ref,
    kernel_ref,
    codes_ref,
    index_ref,
    field,
    own_ref,
    resident_ref,
    sems,
):
    rows, length = out_ref.shape[2], out_ref.shape[3]
    slots, planes = codes_ref.shape[0], own_ref.shape[1]
    copies = []
    for number, (source, target) in enumerate(((own_hbm, own_ref), (resident_hbm, resident_ref))):
        copy = pltpu.make_async_copy(source, target, sems.at[number])
        copy.start()
        copies.append(copy)
    index_ref[0] = counts_ref[0, 0] + counts_ref[0, 1] - 2
    place = lax.axis_index("grid")
    first = lax.broadcasted_iota(jnp.int32, (length, length), 0)
    last = lax.broadcasted_iota(jnp.int32, (length, length), 1)
    first = jnp.minimum(first, length - first).astype(F32)
    last = jnp.minimum(last, length - last).astype(F32)
    around = first * first + last * last
    for row in range(rows):
        middle = place * rows + row
        middle = jnp.minimum(middle, length - middle).astype(F32)
        squared = around + middle * middle
        kernel_ref[:, row * length : (row + 1) * length] = jnp.where(
            squared > 0.5, 0.25 * length**1.5 / jnp.maximum(squared, 1.0), 0.0
        )
    for copy in copies:
        copy.wait()

    def transform(slot):
        forward_slot(
            own_ref,
            lists_ref[0, 0, slot, 0],
            resident_ref,
            lists_ref[0, 0, slot, 1],
            right_ref,
            left_ref,
            out_ref,
            slot * planes,
            field,
            codes_ref.at[slot],
        )

    transform(0)
    for slot in range(1, slots):

        @pl.when(slot < counts_ref[0, 0])
        def _():
            transform(slot)


def late_kernel(
    slots,
    lists_ref,
    counts_ref,
    own_ref,
    received_ref,
    early_ref,
    early_codes_ref,
    right_ref,
    left_ref,
    out_ref,
    field,
    codes,
):
    planes = own_ref.shape[1]

    def transform(number, slot):
        forward_slot(
            own_ref,
            lists_ref[0, 1, number, 0],
            received_ref,
            lists_ref[0, 1, number, 1],
            right_ref,
            left_ref,
            out_ref,
            slot * planes,
            field,
            codes.at[slot],
        )

    def take(number, slot):
        out_ref[:, slot * planes : (slot + 1) * planes] = early_ref[
            :, number * planes : (number + 1) * planes
        ]
        codes[slot] = early_codes_ref[number]

    take(0, 0)
    transform(0, 1)
    if slots == 3:

        @pl.when(counts_ref[0, 0] == 2)
        def _():
            take(1, 2)

        @pl.when(counts_ref[0, 0] != 2)
        def _():
            transform(1, 2)

    if slots == 4:
        take(1, 2)
        transform(1, 3)
    for number, tile in enumerate(packed_codes([codes[slot] for slot in range(slots)], OUT_SHARE)):
        store_tile(out_ref, slots * planes + number, tile)


def middle_kernel(slots, planes, got_ref, kernel_ref, left_ref, out_ref, before, after, codes):
    pieces, rows = got_ref.shape[0], got_ref.shape[2]
    length = pieces * planes
    for slot in range(slots):
        tile = load_tile(got_ref, slots * planes + slot // OUT_SHARE)
        codes[slot] = unpacked_scale(tile, slot % OUT_SHARE, OUT_SHARE)
    for slot in range(slots):
        for piece in range(pieces):
            scale = codes[slot, pl.ds(piece * rows, rows), :]
            for plane in range(planes):
                start = (piece * planes + plane) * rows
                before[slot, pl.ds(start, rows), :] = (
                    got_ref[piece, slot * planes + plane].astype(jnp.int32).astype(F32) * scale
                )
        for pair in range(rows // 2):
            lines = jnp.concatenate(
                [before[slot, pl.ds(pair * 2 + side, length, stride=rows), :] for side in range(2)],
                axis=1,
            )
            lines = from_left(lines, left_ref[...])
            lines = lines * kernel_ref[:, pair * 2 * length : (pair + 1) * 2 * length]
            lines = from_left(lines, left_ref[...])
            for side in range(2):
                after[slot, pl.ds(pair * 2 + side, length, stride=rows), :] = lines[
                    :, side * length : (side + 1) * length
                ]
        for piece in range(pieces):
            codes[slot, pl.ds(piece * rows, rows), :] = encode(
                lambda plane: after[slot, pl.ds((piece * planes + plane) * rows, rows), :],
                store_coded(out_ref, piece, slot * planes),
                planes,
                False,
                BACK_SHARE,
            )
    for number, tile in enumerate(packed_codes([codes[slot] for slot in range(slots)], BACK_SHARE)):
        store_tile(out_ref, slots * planes + number, tile)


def slot_table(lists_ref, counts_ref, slots):
    table = []
    for slot in range(slots):
        if slot < 2:
            which, place = slot, 0
        elif slots == 3:
            which, place = jnp.where(counts_ref[0, 0] == 2, 0, 1), 1
        else:
            which, place = slot - 2, 1
        table.append((which, lists_ref[0, which, place, 0], lists_ref[0, which, place, 1]))
    return table


def partner_plane(resident_ref, received_ref, which, band, plane):
    if isinstance(which, int):
        chosen = received_ref if which else resident_ref
        return chosen[band, plane].astype(F32)
    return jnp.where(
        which == 1, received_ref[band, plane].astype(F32), resident_ref[band, plane].astype(F32)
    )


def final_kernel(
    slots,
    lists_ref,
    counts_ref,
    own_ref,
    resident_ref,
    received_ref,
    got_ref,
    right_ref,
    left_ref,
    out_hbm,
    terms_ref,
    scales,
    sums,
    out_ref,
    sems,
):
    table = slot_table(lists_ref, counts_ref, slots)
    bands, planes, length = own_ref.shape[:3]
    for slot in range(slots):
        tile = load_tile(got_ref, slots * planes + slot // BACK_SHARE)
        scales[slot] = unpacked_scale(tile, slot % BACK_SHARE, BACK_SHARE)
    sums[...] = jnp.zeros_like(sums)

    def copies(pair):
        return [
            pltpu.make_async_copy(
                out_ref.at[band, pl.ds(pair * 2, 2)],
                out_hbm.at[band, pl.ds(pair * 2, 2)],
                sems.at[pair, band],
            )
            for band in range(bands)
        ]

    for pair in range(planes // 2):
        totals = [[jnp.zeros((length, length), F32) for _ in range(bands)] for _ in range(2)]
        for slot, (which, first, second) in enumerate(table):
            lines = []
            for side in range(2):
                value = load_tile(got_ref, slot * planes + pair * 2 + side)
                lines.append(value * scales[slot])
            lines = from_left(jnp.concatenate(lines, axis=1), left_ref[...])
            lines = jnp.concatenate([lines[:, :length], lines[:, length:]], axis=0)
            lines = from_right(lines, right_ref[...])
            for side in range(2):
                plane = pair * 2 + side
                term = lines[side * length : (side + 1) * length] * partner_plane(
                    resident_ref, received_ref, which, second, plane
                )
                for band in range(bands):
                    totals[side][band] += jnp.where(first == band, term, 0.0)
        for side in range(2):
            plane = pair * 2 + side
            for band in range(bands):
                out_ref[band, plane] = totals[side][band].astype(out_ref.dtype)
                for other in range(bands):
                    product = own_ref[other, plane].astype(F32) * totals[side][band]
                    sums[other * bands + band] += product.reshape(length // 8, 8, length).sum(axis=0)
        if pair:
            for copy in copies(pair - 1):
                copy.start()

    for entry in range(bands * bands):
        row = jnp.sum(sums[entry], axis=0, keepdims=True)
        terms_ref[:, entry // bands, entry % bands : entry % bands + 1, :] = jnp.broadcast_to(
            row[None], (terms_ref.shape[0], 1, row.shape[1])
        )
    for copy in copies(planes // 2 - 1):
        copy.start()
    for pair in range(planes // 2):
        for copy in copies(pair):
            copy.wait()


VMEM = pl.BlockSpec(memory_space=pltpu.VMEM)
SMEM = pl.BlockSpec(memory_space=pltpu.SMEM)
ANY = pl.BlockSpec(memory_space=pl.ANY)


def on_device(right, left, own_orbitals, resident_orbitals, pair_lists, pair_counts):
    bands, planes, length = own_orbitals.shape[:3]
    pieces = lax.axis_size("grid")
    rows = length // pieces
    received = passed_along(resident_orbitals, "band", 1)
    lists, counts = pair_lists, pair_counts
    field = pltpu.VMEM((planes, length, length), F32)

    table = pltpu.VMEM((4, length, length), F32)

    def coded(slots, share):
        tiles = slots * planes + (-(-slots // share) if share else 0)
        return jax.ShapeDtypeStruct((pieces, tiles, rows, length), jnp.int16)

    early, kernel, codes, index = pl.pallas_call(
        early_kernel,
        out_shape=(
            coded(2, 0),
            jax.ShapeDtypeStruct((length, rows * length), F32),
            jax.ShapeDtypeStruct((2, length, length), F32),
            jax.ShapeDtypeStruct((1,), jnp.int32),
        ),
        in_specs=[SMEM, SMEM, ANY, ANY, VMEM, VMEM],
        out_specs=(VMEM, VMEM, VMEM, SMEM),
        scratch_shapes=[
            field,
            pltpu.VMEM(own_orbitals.shape, BF16),
            pltpu.VMEM(own_orbitals.shape, BF16),
            pltpu.SemaphoreType.DMA((2,)),
        ],
        cost_estimate=pl.CostEstimate(
            flops=600_000_000, bytes_accessed=3_000_000, transcendentals=0
        ),
        compiler_params=LIMIT,
        name="early",
    )(lists, counts, own_orbitals, resident_orbitals, right, left)

    def branch(slots):
        def run(own_orbitals, resident_orbitals, received, lists, counts, early, kernel, codes, right, left):
            sent = pl.pallas_call(
                functools.partial(late_kernel, slots),
                out_shape=coded(slots, OUT_SHARE),
                in_specs=[SMEM, SMEM, VMEM, VMEM, VMEM, VMEM, VMEM, VMEM],
                out_specs=VMEM,
                scratch_shapes=[field, table],
                compiler_params=LIMIT,
                name="late",
            )(lists, counts, own_orbitals, received, early, codes, right, left)
            got = lax.all_to_all(sent, "grid", split_axis=0, concat_axis=0, tiled=True)
            sent = pl.pallas_call(
                functools.partial(middle_kernel, slots, planes),
                out_shape=coded(slots, BACK_SHARE),
                in_specs=[VMEM, VMEM, VMEM],
                out_specs=VMEM,
                scratch_shapes=[pltpu.VMEM((slots, length * rows, length), F32)] * 2 + [table],
                compiler_params=LIMIT,
                name="middle",
            )(got, kernel, left)
            got = lax.all_to_all(sent, "grid", split_axis=0, concat_axis=0, tiled=True)
            return pl.pallas_call(
                functools.partial(final_kernel, slots),
                out_shape=(
                    jax.ShapeDtypeStruct(own_orbitals.shape, BF16),
                    jax.ShapeDtypeStruct((pieces, bands, bands, length), F32),
                ),
                in_specs=[SMEM, SMEM, VMEM, VMEM, VMEM, VMEM, VMEM, VMEM],
                out_specs=(ANY, VMEM),
                scratch_shapes=[
                    pltpu.VMEM((slots, length, length), F32),
                    pltpu.VMEM((bands * bands, 8, length), F32),
                    pltpu.VMEM(own_orbitals.shape, BF16),
                    pltpu.SemaphoreType.DMA((planes // 2, bands)),
                ],
                compiler_params=LIMIT,
                name="final",
            )(lists, counts, own_orbitals, resident_orbitals, received, got, right, left)

        return run

    exchange, terms = lax.switch(
        index[0],
        [branch(2), branch(3), branch(4)],
        own_orbitals,
        resident_orbitals,
        received,
        lists,
        counts,
        early,
        kernel,
        codes,
        right,
        left,
    )
    terms = lax.all_to_all(terms, "grid", split_axis=0, concat_axis=0, tiled=True)
    return exchange, jnp.sum(terms, axis=(0, 3))


def solution(mesh):
    in_specs = (
        P(None, None),
        P(None, None),
        P("band", "grid", None, None),
        P("band", "grid", None, None),
        P("band", None, None, None),
        P("band", None),
    )
    out_specs = (P("band", "grid", None, None), P("band", None))
    mapped = jax.shard_map(
        on_device, mesh=mesh, in_specs=in_specs, out_specs=out_specs, check_vma=False
    )

    def step(own_orbitals, resident_orbitals, pair_lists, pair_counts):
        length = own_orbitals.shape[-1]
        right, left = jnp.asarray(right_table(length)), jnp.asarray(left_table(length))
        return mapped(right, left, own_orbitals, resident_orbitals, pair_lists, pair_counts)

    return step
```

```python
import functools
import math

import jax
import jax.numpy as jnp
import numpy as np
from jax import lax
from jax.experimental import pallas as pl
from jax.experimental.pallas import tpu as pltpu
from jax.sharding import PartitionSpec as P

BF16 = jnp.bfloat16
F32 = jnp.float32
TOP = 32760.0
STEPS = 256.0
FLOOR = 2.0**-110
GROUP = 4
OUT_SHARE = 4
BACK_SHARE = 2
LIMIT = pltpu.CompilerParams(vmem_limit_bytes=20 << 20)


def passed_along(x, axis, by):
    length = lax.axis_size(axis)
    return lax.ppermute(x, axis, [(i, (i + by) % length) for i in range(length)])


def cas_halves(length):
    indices = np.arange(length)
    angles = (indices[:, None] * indices[None, :] % length) * (2.0 * math.pi / length)
    table = (np.cos(angles) + np.sin(angles)) / math.sqrt(length)
    high = table.astype(np.float32).astype(BF16)
    low = (table - high.astype(np.float64)).astype(np.float32).astype(BF16)
    return high, low


def right_table(length):
    high, low = cas_halves(length)
    row = np.concatenate([high, low], axis=1)
    return np.concatenate([row, row], axis=0)


def left_table(length):
    high, low = cas_halves(length)
    column = np.concatenate([high, low], axis=0)
    return np.concatenate([column, column], axis=1)


def halves(x):
    high = x.astype(BF16)
    return high, (x - high.astype(F32)).astype(BF16)


def from_right(x, table):
    half = x.shape[1]
    both = jnp.dot(jnp.concatenate(halves(x), axis=1), table, preferred_element_type=F32)
    return both[:, :half] + both[:, half:]


def from_left(x, table):
    half = x.shape[0]
    both = jnp.dot(table, jnp.concatenate(halves(x), axis=0), preferred_element_type=F32)
    return both[:half] + both[half:]


def scale_code(peak):
    return jnp.ceil(jnp.log2(jnp.maximum(peak, FLOOR)) * STEPS)


def decoded_scale(code):
    return jnp.exp2(code * (1.0 / STEPS)) * (1.0 / TOP)


def lane_group(shape, share):
    return lax.broadcasted_iota(jnp.int32, shape, 1) // (shape[1] // share)


def over_lanes(x, share, combine):
    step = x.shape[1]
    while share > 1:
        step, share = step // 2, share // 2
        x = combine(x, pltpu.roll(x, step, 1))
    return x


def packed_codes(codes, share):
    tiles = []
    for start in range(0, len(codes), share):
        tile = codes[start]
        group = lane_group(tile.shape, share)
        for offset, code in enumerate(codes[start + 1 : start + share]):
            tile = jnp.where(group == offset + 1, code, tile)
        tiles.append(tile)
    return tiles


def unpacked_scale(tile, place, share):
    group = lane_group(tile.shape, share)
    return decoded_scale(over_lanes(jnp.where(group == place, tile, 0.0), share, jnp.add))


def encode(load, store, planes, carry, share):
    values = [load(plane) for plane in range(planes)]
    peak = functools.reduce(jnp.maximum, [jnp.abs(value) for value in values])
    code = scale_code(over_lanes(peak, share, jnp.maximum))
    inverse = jnp.exp2(code * (-1.0 / STEPS)) * TOP
    left = None
    for plane, value in enumerate(values):
        scaled = value * inverse
        if left is not None:
            scaled = scaled + left
        whole = jnp.round(scaled)
        if carry:
            left = scaled - whole
        store(plane, whole.astype(jnp.int32))
    return code


def store_coded(out_ref, piece, first):
    rows = out_ref.shape[2]

    def store(plane, value):
        count = value.shape[0] // rows
        value = value.reshape(count, rows, value.shape[1]).astype(jnp.int16)
        out_ref[pl.ds(piece, count), first + plane] = value

    return store


def store_tile(out_ref, number, tile):
    pieces, _, rows, length = out_ref.shape
    out_ref[:, number] = tile.astype(jnp.int32).reshape(pieces, rows, length).astype(jnp.int16)


def load_tile(got_ref, number):
    pieces, _, rows, length = got_ref.shape
    return got_ref[:, number].astype(jnp.int32).astype(F32).reshape(pieces * rows, length)


def forward_slot(own_ref, first, partner_ref, second, right_ref, left_ref, out_ref, start, field, code_ref):
    planes, length = own_ref.shape[1], own_ref.shape[2]
    pieces, rows = out_ref.shape[0], out_ref.shape[2]
    for pair in range(planes // 2):
        densities = [
            own_ref[first, plane].astype(F32) * partner_ref[second, plane].astype(F32)
            for plane in (pair * 2, pair * 2 + 1)
        ]
        lines = from_right(jnp.concatenate(densities, axis=0), right_ref[...])
        lines = jnp.concatenate([lines[:length], lines[length:]], axis=1)
        lines = from_left(lines, left_ref[...])
        for side in range(2):
            field[pair * 2 + side] = lines[:, side * length : (side + 1) * length]
    for piece in range(0, pieces, GROUP):
        code_ref[pl.ds(piece * rows, GROUP * rows), :] = encode(
            lambda plane: field[plane, pl.ds(piece * rows, GROUP * rows), :],
            store_coded(out_ref, piece, start),
            planes,
            True,
            OUT_SHARE,
        )


def early_kernel(
    lists_ref,
    counts_ref,
    own_hbm,
    resident_hbm,
    right_ref,
    left_ref,
    out_ref,
    kernel_ref,
    codes_ref,
    index_ref,
    field,
    own_ref,
    resident_ref,
    sems,
):
    rows, length = out_ref.shape[2], out_ref.shape[3]
    slots, planes = codes_ref.shape[0], own_ref.shape[1]
    copies = []
    for number, (source, target) in enumerate(((own_hbm, own_ref), (resident_hbm, resident_ref))):
        copy = pltpu.make_async_copy(source, target, sems.at[number])
        copy.start()
        copies.append(copy)
    index_ref[0] = counts_ref[0, 0] + counts_ref[0, 1] - 2
    place = lax.axis_index("grid")
    first = lax.broadcasted_iota(jnp.int32, (length, length), 0)
    last = lax.broadcasted_iota(jnp.int32, (length, length), 1)
    first = jnp.minimum(first, length - first).astype(F32)
    last = jnp.minimum(last, length - last).astype(F32)
    around = first * first + last * last
    for row in range(rows):
        middle = place * rows + row
        middle = jnp.minimum(middle, length - middle).astype(F32)
        squared = around + middle * middle
        kernel_ref[:, row * length : (row + 1) * length] = jnp.where(
            squared > 0.5, 0.25 * length**1.5 / jnp.maximum(squared, 1.0), 0.0
        )
    for copy in copies:
        copy.wait()

    def transform(slot):
        forward_slot(
            own_ref,
            lists_ref[0, 0, slot, 0],
            resident_ref,
            lists_ref[0, 0, slot, 1],
            right_ref,
            left_ref,
            out_ref,
            slot * planes,
            field,
            codes_ref.at[slot],
        )

    transform(0)
    for slot in range(1, slots):

        @pl.when(slot < counts_ref[0, 0])
        def _():
            transform(slot)


def late_kernel(
    slots,
    lists_ref,
    counts_ref,
    own_ref,
    received_ref,
    early_ref,
    early_codes_ref,
    right_ref,
    left_ref,
    out_ref,
    fields,
    codes,
):
    planes = own_ref.shape[1]

    def transform(number, slot):
        forward_slot(
            own_ref,
            lists_ref[0, 1, number, 0],
            received_ref,
            lists_ref[0, 1, number, 1],
            right_ref,
            left_ref,
            out_ref,
            slot * planes,
            fields.at[number],
            codes.at[slot],
        )

    def take(number, slot):
        out_ref[:, slot * planes : (slot + 1) * planes] = early_ref[
            :, number * planes : (number + 1) * planes
        ]
        codes[slot] = early_codes_ref[number]

    take(0, 0)
    if slots == 3:

        @pl.when(counts_ref[0, 0] == 2)
        def _():
            take(1, 2)
            transform(0, 1)

        @pl.when(counts_ref[0, 0] != 2)
        def _():
            transform(0, 1)
            transform(1, 2)

    else:
        transform(0, 1)
    if slots == 4:
        take(1, 2)
        transform(1, 3)
    for number, tile in enumerate(packed_codes([codes[slot] for slot in range(slots)], OUT_SHARE)):
        store_tile(out_ref, slots * planes + number, tile)


def middle_kernel(slots, planes, got_ref, kernel_ref, left_ref, out_ref, before, after, codes):
    pieces, rows = got_ref.shape[0], got_ref.shape[2]
    length = pieces * planes
    for slot in range(slots):
        tile = load_tile(got_ref, slots * planes + slot // OUT_SHARE)
        codes[slot] = unpacked_scale(tile, slot % OUT_SHARE, OUT_SHARE)
    for slot in range(slots):
        for piece in range(pieces):
            scale = codes[slot, pl.ds(piece * rows, rows), :]
            for plane in range(planes):
                start = (piece * planes + plane) * rows
                before[slot, pl.ds(start, rows), :] = (
                    got_ref[piece, slot * planes + plane].astype(jnp.int32).astype(F32) * scale
                )
        for pair in range(rows // 2):
            lines = jnp.concatenate(
                [before[slot, pl.ds(pair * 2 + side, length, stride=rows), :] for side in range(2)],
                axis=1,
            )
            lines = from_left(lines, left_ref[...])
            lines = lines * kernel_ref[:, pair * 2 * length : (pair + 1) * 2 * length]
            lines = from_left(lines, left_ref[...])
            for side in range(2):
                after[slot, pl.ds(pair * 2 + side, length, stride=rows), :] = lines[
                    :, side * length : (side + 1) * length
                ]
        for piece in range(pieces):
            codes[slot, pl.ds(piece * rows, rows), :] = encode(
                lambda plane: after[slot, pl.ds((piece * planes + plane) * rows, rows), :],
                store_coded(out_ref, piece, slot * planes),
                planes,
                False,
                BACK_SHARE,
            )
    for number, tile in enumerate(packed_codes([codes[slot] for slot in range(slots)], BACK_SHARE)):
        store_tile(out_ref, slots * planes + number, tile)


def slot_table(lists_ref, counts_ref, slots):
    table = []
    for slot in range(slots):
        if slot < 2:
            which, place = slot, 0
        elif slots == 3:
            which, place = jnp.where(counts_ref[0, 0] == 2, 0, 1), 1
        else:
            which, place = slot - 2, 1
        table.append((which, lists_ref[0, which, place, 0], lists_ref[0, which, place, 1]))
    return table


def partner_plane(resident_ref, received_ref, which, band, plane):
    if isinstance(which, int):
        chosen = received_ref if which else resident_ref
        return chosen[band, plane].astype(F32)
    return jnp.where(
        which == 1, received_ref[band, plane].astype(F32), resident_ref[band, plane].astype(F32)
    )


def final_kernel(
    slots,
    lists_ref,
    counts_ref,
    own_ref,
    resident_ref,
    received_ref,
    got_ref,
    right_ref,
    left_ref,
    out_hbm,
    terms_ref,
    scales,
    sums,
    out_ref,
    sems,
):
    table = slot_table(lists_ref, counts_ref, slots)
    bands, planes, length = own_ref.shape[:3]
    for slot in range(slots):
        tile = load_tile(got_ref, slots * planes + slot // BACK_SHARE)
        scales[slot] = unpacked_scale(tile, slot % BACK_SHARE, BACK_SHARE)
    sums[...] = jnp.zeros_like(sums)

    def copies(pair):
        return [
            pltpu.make_async_copy(
                out_ref.at[band, pl.ds(pair * 2, 2)],
                out_hbm.at[band, pl.ds(pair * 2, 2)],
                sems.at[pair, band],
            )
            for band in range(bands)
        ]

    for pair in range(planes // 2):
        totals = [[jnp.zeros((length, length), F32) for _ in range(bands)] for _ in range(2)]
        for slot, (which, first, second) in enumerate(table):
            lines = []
            for side in range(2):
                value = load_tile(got_ref, slot * planes + pair * 2 + side)
                lines.append(value * scales[slot])
            lines = from_left(jnp.concatenate(lines, axis=1), left_ref[...])
            lines = jnp.concatenate([lines[:, :length], lines[:, length:]], axis=0)
            lines = from_right(lines, right_ref[...])
            for side in range(2):
                plane = pair * 2 + side
                term = lines[side * length : (side + 1) * length] * partner_plane(
                    resident_ref, received_ref, which, second, plane
                )
                for band in range(bands):
                    totals[side][band] += jnp.where(first == band, term, 0.0)
        for side in range(2):
            plane = pair * 2 + side
            for band in range(bands):
                out_ref[band, plane] = totals[side][band].astype(out_ref.dtype)
                for other in range(bands):
                    product = own_ref[other, plane].astype(F32) * totals[side][band]
                    sums[other * bands + band] += product.reshape(length // 8, 8, length).sum(axis=0)
        if pair:
            for copy in copies(pair - 1):
                copy.start()

    for entry in range(bands * bands):
        row = jnp.sum(sums[entry], axis=0, keepdims=True)
        terms_ref[:, entry // bands, entry % bands : entry % bands + 1, :] = jnp.broadcast_to(
            row[None], (terms_ref.shape[0], 1, row.shape[1])
        )
    for copy in copies(planes // 2 - 1):
        copy.start()
    for pair in range(planes // 2):
        for copy in copies(pair):
            copy.wait()


VMEM = pl.BlockSpec(memory_space=pltpu.VMEM)
SMEM = pl.BlockSpec(memory_space=pltpu.SMEM)
ANY = pl.BlockSpec(memory_space=pl.ANY)


def on_device(right, left, own_orbitals, resident_orbitals, pair_lists, pair_counts):
    bands, planes, length = own_orbitals.shape[:3]
    pieces = lax.axis_size("grid")
    rows = length // pieces
    received = passed_along(resident_orbitals, "band", 1)
    lists, counts = pair_lists, pair_counts
    field = pltpu.VMEM((planes, length, length), F32)

    table = pltpu.VMEM((4, length, length), F32)

    def coded(slots, share):
        tiles = slots * planes + (-(-slots // share) if share else 0)
        return jax.ShapeDtypeStruct((pieces, tiles, rows, length), jnp.int16)

    early, kernel, codes, index = pl.pallas_call(
        early_kernel,
        out_shape=(
            coded(2, 0),
            jax.ShapeDtypeStruct((length, rows * length), F32),
            jax.ShapeDtypeStruct((2, length, length), F32),
            jax.ShapeDtypeStruct((1,), jnp.int32),
        ),
        in_specs=[SMEM, SMEM, ANY, ANY, VMEM, VMEM],
        out_specs=(VMEM, VMEM, VMEM, SMEM),
        scratch_shapes=[
            field,
            pltpu.VMEM(own_orbitals.shape, BF16),
            pltpu.VMEM(own_orbitals.shape, BF16),
            pltpu.SemaphoreType.DMA((2,)),
        ],
        cost_estimate=pl.CostEstimate(
            flops=600_000_000, bytes_accessed=3_000_000, transcendentals=0
        ),
        compiler_params=LIMIT,
        name="early",
    )(lists, counts, own_orbitals, resident_orbitals, right, left)

    def branch(slots):
        def run(own_orbitals, resident_orbitals, received, lists, counts, early, kernel, codes, right, left):
            sent = pl.pallas_call(
                functools.partial(late_kernel, slots),
                out_shape=coded(slots, OUT_SHARE),
                in_specs=[SMEM, SMEM, VMEM, VMEM, VMEM, VMEM, VMEM, VMEM],
                out_specs=VMEM,
                scratch_shapes=[pltpu.VMEM((2, planes, length, length), F32), table],
                compiler_params=LIMIT,
                name="late",
            )(lists, counts, own_orbitals, received, early, codes, right, left)
            got = lax.all_to_all(sent, "grid", split_axis=0, concat_axis=0, tiled=True)
            sent = pl.pallas_call(
                functools.partial(middle_kernel, slots, planes),
                out_shape=coded(slots, BACK_SHARE),
                in_specs=[VMEM, VMEM, VMEM],
                out_specs=VMEM,
                scratch_shapes=[pltpu.VMEM((slots, length * rows, length), F32)] * 2 + [table],
                compiler_params=LIMIT,
                name="middle",
            )(got, kernel, left)
            got = lax.all_to_all(sent, "grid", split_axis=0, concat_axis=0, tiled=True)
            return pl.pallas_call(
                functools.partial(final_kernel, slots),
                out_shape=(
                    jax.ShapeDtypeStruct(own_orbitals.shape, BF16),
                    jax.ShapeDtypeStruct((pieces, bands, bands, length), F32),
                ),
                in_specs=[SMEM, SMEM, VMEM, VMEM, VMEM, VMEM, VMEM, VMEM],
                out_specs=(ANY, VMEM),
                scratch_shapes=[
                    pltpu.VMEM((slots, length, length), F32),
                    pltpu.VMEM((bands * bands, 8, length), F32),
                    pltpu.VMEM(own_orbitals.shape, BF16),
                    pltpu.SemaphoreType.DMA((planes // 2, bands)),
                ],
                compiler_params=LIMIT,
                name="final",
            )(lists, counts, own_orbitals, resident_orbitals, received, got, right, left)

        return run

    exchange, terms = lax.switch(
        index[0],
        [branch(2), branch(3), branch(4)],
        own_orbitals,
        resident_orbitals,
        received,
        lists,
        counts,
        early,
        kernel,
        codes,
        right,
        left,
    )
    terms = lax.all_to_all(terms, "grid", split_axis=0, concat_axis=0, tiled=True)
    return exchange, jnp.sum(terms, axis=(0, 3))


def solution(mesh):
    in_specs = (
        P(None, None),
        P(None, None),
        P("band", "grid", None, None),
        P("band", "grid", None, None),
        P("band", None, None, None),
        P("band", None),
    )
    out_specs = (P("band", "grid", None, None), P("band", None))
    mapped = jax.shard_map(
        on_device, mesh=mesh, in_specs=in_specs, out_specs=out_specs, check_vma=False
    )

    def step(own_orbitals, resident_orbitals, pair_lists, pair_counts):
        length = own_orbitals.shape[-1]
        right, left = jnp.asarray(right_table(length)), jnp.asarray(left_table(length))
        return mapped(right, left, own_orbitals, resident_orbitals, pair_lists, pair_counts)

    return step
```

```python
import functools
import math

import jax
import jax.numpy as jnp
import numpy as np
from jax import lax
from jax.experimental import pallas as pl
from jax.experimental.pallas import tpu as pltpu
from jax.sharding import PartitionSpec as P

BF16 = jnp.bfloat16
F32 = jnp.float32
TOP = 32760.0
STEPS = 256.0
FLOOR = 2.0**-110
GROUP = 4
OUT_SHARE = 4
BACK_SHARE = 4
LIMIT = pltpu.CompilerParams(vmem_limit_bytes=20 << 20)


def passed_along(x, axis, by):
    length = lax.axis_size(axis)
    return lax.ppermute(x, axis, [(i, (i + by) % length) for i in range(length)])


def cas_halves(length):
    indices = np.arange(length)
    angles = (indices[:, None] * indices[None, :] % length) * (2.0 * math.pi / length)
    table = (np.cos(angles) + np.sin(angles)) / math.sqrt(length)
    high = table.astype(np.float32).astype(BF16)
    low = (table - high.astype(np.float64)).astype(np.float32).astype(BF16)
    return high, low


def right_table(length):
    high, low = cas_halves(length)
    row = np.concatenate([high, low], axis=1)
    return np.concatenate([row, row], axis=0)


def left_table(length):
    high, low = cas_halves(length)
    column = np.concatenate([high, low], axis=0)
    return np.concatenate([column, column], axis=1)


def halves(x):
    high = x.astype(BF16)
    return high, (x - high.astype(F32)).astype(BF16)


def from_right(x, table):
    half = x.shape[1]
    both = jnp.dot(jnp.concatenate(halves(x), axis=1), table, preferred_element_type=F32)
    return both[:, :half] + both[:, half:]


def from_left(x, table):
    half = x.shape[0]
    both = jnp.dot(table, jnp.concatenate(halves(x), axis=0), preferred_element_type=F32)
    return both[:half] + both[half:]


def scale_code(peak):
    return jnp.ceil(jnp.log2(jnp.maximum(peak, FLOOR)) * STEPS)


def decoded_scale(code):
    return jnp.exp2(code * (1.0 / STEPS)) * (1.0 / TOP)


def lane_group(shape, share):
    return lax.broadcasted_iota(jnp.int32, shape, 1) // (shape[1] // share)


def over_lanes(x, share, combine):
    step = x.shape[1]
    while share > 1:
        step, share = step // 2, share // 2
        x = combine(x, pltpu.roll(x, step, 1))
    return x


def packed_codes(codes, share):
    tiles = []
    for start in range(0, len(codes), share):
        tile = codes[start]
        group = lane_group(tile.shape, share)
        for offset, code in enumerate(codes[start + 1 : start + share]):
            tile = jnp.where(group == offset + 1, code, tile)
        tiles.append(tile)
    return tiles


def unpacked_scale(tile, place, share):
    group = lane_group(tile.shape, share)
    return decoded_scale(over_lanes(jnp.where(group == place, tile, 0.0), share, jnp.add))


def encode(load, store, planes, carry, share):
    values = [load(plane) for plane in range(planes)]
    peak = functools.reduce(jnp.maximum, [jnp.abs(value) for value in values])
    code = scale_code(over_lanes(peak, share, jnp.maximum))
    inverse = jnp.exp2(code * (-1.0 / STEPS)) * TOP
    left = None
    for plane, value in enumerate(values):
        scaled = value * inverse
        if left is not None:
            scaled = scaled + left
        whole = jnp.round(scaled)
        if carry:
            left = scaled - whole
        store(plane, whole.astype(jnp.int32))
    return code


def store_coded(out_ref, piece, first):
    rows = out_ref.shape[2]

    def store(plane, value):
        count = value.shape[0] // rows
        value = value.reshape(count, rows, value.shape[1]).astype(jnp.int16)
        out_ref[pl.ds(piece, count), first + plane] = value

    return store


def store_tile(out_ref, number, tile):
    pieces, _, rows, length = out_ref.shape
    out_ref[:, number] = tile.astype(jnp.int32).reshape(pieces, rows, length).astype(jnp.int16)


def load_tile(got_ref, number):
    pieces, _, rows, length = got_ref.shape
    return got_ref[:, number].astype(jnp.int32).astype(F32).reshape(pieces * rows, length)


def forward_slot(own_ref, first, partner_ref, second, right_ref, left_ref, out_ref, start, field, code_ref):
    planes, length = own_ref.shape[1], own_ref.shape[2]
    pieces, rows = out_ref.shape[0], out_ref.shape[2]
    for pair in range(planes // 2):
        densities = [
            own_ref[first, plane].astype(F32) * partner_ref[second, plane].astype(F32)
            for plane in (pair * 2, pair * 2 + 1)
        ]
        lines = from_right(jnp.concatenate(densities, axis=0), right_ref[...])
        lines = jnp.concatenate([lines[:length], lines[length:]], axis=1)
        lines = from_left(lines, left_ref[...])
        for side in range(2):
            field[pair * 2 + side] = lines[:, side * length : (side + 1) * length]
    for piece in range(0, pieces, GROUP):
        code_ref[pl.ds(piece * rows, GROUP * rows), :] = encode(
            lambda plane: field[plane, pl.ds(piece * rows, GROUP * rows), :],
            store_coded(out_ref, piece, start),
            planes,
            True,
            OUT_SHARE,
        )


def early_kernel(
    lists_ref,
    counts_ref,
    own_hbm,
    resident_hbm,
    right_ref,
    left_ref,
    out_ref,
    kernel_ref,
    codes_ref,
    index_ref,
    field,
    own_ref,
    resident_ref,
    sems,
):
    rows, length = out_ref.shape[2], out_ref.shape[3]
    slots, planes = codes_ref.shape[0], own_ref.shape[1]
    copies = []
    for number, (source, target) in enumerate(((own_hbm, own_ref), (resident_hbm, resident_ref))):
        copy = pltpu.make_async_copy(source, target, sems.at[number])
        copy.start()
        copies.append(copy)
    index_ref[0] = counts_ref[0, 0] + counts_ref[0, 1] - 2
    place = lax.axis_index("grid")
    first = lax.broadcasted_iota(jnp.int32, (length, length), 0)
    last = lax.broadcasted_iota(jnp.int32, (length, length), 1)
    first = jnp.minimum(first, length - first).astype(F32)
    last = jnp.minimum(last, length - last).astype(F32)
    around = first * first + last * last
    for row in range(rows):
        middle = place * rows + row
        middle = jnp.minimum(middle, length - middle).astype(F32)
        squared = around + middle * middle
        kernel_ref[:, row * length : (row + 1) * length] = jnp.where(
            squared > 0.5, 0.25 * length**1.5 / jnp.maximum(squared, 1.0), 0.0
        )
    for copy in copies:
        copy.wait()

    def transform(slot):
        forward_slot(
            own_ref,
            lists_ref[0, 0, slot, 0],
            resident_ref,
            lists_ref[0, 0, slot, 1],
            right_ref,
            left_ref,
            out_ref,
            slot * planes,
            field,
            codes_ref.at[slot],
        )

    transform(0)
    for slot in range(1, slots):

        @pl.when(slot < counts_ref[0, 0])
        def _():
            transform(slot)


def late_kernel(
    slots,
    lists_ref,
    counts_ref,
    own_ref,
    received_ref,
    early_ref,
    early_codes_ref,
    right_ref,
    left_ref,
    out_ref,
    fields,
    codes,
):
    planes = own_ref.shape[1]

    def transform(number, slot):
        forward_slot(
            own_ref,
            lists_ref[0, 1, number, 0],
            received_ref,
            lists_ref[0, 1, number, 1],
            right_ref,
            left_ref,
            out_ref,
            slot * planes,
            fields.at[number],
            codes.at[slot],
        )

    def take(number, slot):
        out_ref[:, slot * planes : (slot + 1) * planes] = early_ref[
            :, number * planes : (number + 1) * planes
        ]
        codes[slot] = early_codes_ref[number]

    take(0, 0)
    if slots == 3:

        @pl.when(counts_ref[0, 0] == 2)
        def _():
            take(1, 2)
            transform(0, 1)

        @pl.when(counts_ref[0, 0] != 2)
        def _():
            transform(0, 1)
            transform(1, 2)

    else:
        transform(0, 1)
    if slots == 4:
        take(1, 2)
        transform(1, 3)
    for number, tile in enumerate(packed_codes([codes[slot] for slot in range(slots)], OUT_SHARE)):
        store_tile(out_ref, slots * planes + number, tile)


def middle_kernel(slots, planes, got_ref, kernel_ref, left_ref, out_ref, before, after, codes):
    pieces, rows = got_ref.shape[0], got_ref.shape[2]
    length = pieces * planes
    for slot in range(slots):
        tile = load_tile(got_ref, slots * planes + slot // OUT_SHARE)
        codes[slot] = unpacked_scale(tile, slot % OUT_SHARE, OUT_SHARE)
    for slot in range(slots):
        for piece in range(pieces):
            scale = codes[slot, pl.ds(piece * rows, rows), :]
            for plane in range(planes):
                start = (piece * planes + plane) * rows
                before[slot, pl.ds(start, rows), :] = (
                    got_ref[piece, slot * planes + plane].astype(jnp.int32).astype(F32) * scale
                )
        for pair in range(rows // 2):
            lines = jnp.concatenate(
                [before[slot, pl.ds(pair * 2 + side, length, stride=rows), :] for side in range(2)],
                axis=1,
            )
            lines = from_left(lines, left_ref[...])
            lines = lines * kernel_ref[:, pair * 2 * length : (pair + 1) * 2 * length]
            lines = from_left(lines, left_ref[...])
            for side in range(2):
                after[slot, pl.ds(pair * 2 + side, length, stride=rows), :] = lines[
                    :, side * length : (side + 1) * length
                ]
        for piece in range(pieces):
            codes[slot, pl.ds(piece * rows, rows), :] = encode(
                lambda plane: after[slot, pl.ds((piece * planes + plane) * rows, rows), :],
                store_coded(out_ref, piece, slot * planes),
                planes,
                False,
                BACK_SHARE,
            )
    for number, tile in enumerate(packed_codes([codes[slot] for slot in range(slots)], BACK_SHARE)):
        store_tile(out_ref, slots * planes + number, tile)


def slot_table(lists_ref, counts_ref, slots):
    table = []
    for slot in range(slots):
        if slot < 2:
            which, place = slot, 0
        elif slots == 3:
            which, place = jnp.where(counts_ref[0, 0] == 2, 0, 1), 1
        else:
            which, place = slot - 2, 1
        table.append((which, lists_ref[0, which, place, 0], lists_ref[0, which, place, 1]))
    return table


def partner_plane(resident_ref, received_ref, which, band, plane):
    if isinstance(which, int):
        chosen = received_ref if which else resident_ref
        return chosen[band, plane].astype(F32)
    return jnp.where(
        which == 1, received_ref[band, plane].astype(F32), resident_ref[band, plane].astype(F32)
    )


def final_kernel(
    slots,
    lists_ref,
    counts_ref,
    own_ref,
    resident_ref,
    received_ref,
    got_ref,
    right_ref,
    left_ref,
    out_hbm,
    terms_ref,
    scales,
    sums,
    out_ref,
    sems,
):
    table = slot_table(lists_ref, counts_ref, slots)
    bands, planes, length = own_ref.shape[:3]
    for slot in range(slots):
        tile = load_tile(got_ref, slots * planes + slot // BACK_SHARE)
        scales[slot] = unpacked_scale(tile, slot % BACK_SHARE, BACK_SHARE)
    sums[...] = jnp.zeros_like(sums)

    def copies(pair):
        return [
            pltpu.make_async_copy(
                out_ref.at[band, pl.ds(pair * 2, 2)],
                out_hbm.at[band, pl.ds(pair * 2, 2)],
                sems.at[pair, band],
            )
            for band in range(bands)
        ]

    for pair in range(planes // 2):
        totals = [[jnp.zeros((length, length), F32) for _ in range(bands)] for _ in range(2)]
        for slot, (which, first, second) in enumerate(table):
            lines = []
            for side in range(2):
                value = load_tile(got_ref, slot * planes + pair * 2 + side)
                lines.append(value * scales[slot])
            lines = from_left(jnp.concatenate(lines, axis=1), left_ref[...])
            lines = jnp.concatenate([lines[:, :length], lines[:, length:]], axis=0)
            lines = from_right(lines, right_ref[...])
            for side in range(2):
                plane = pair * 2 + side
                term = lines[side * length : (side + 1) * length] * partner_plane(
                    resident_ref, received_ref, which, second, plane
                )
                for band in range(bands):
                    totals[side][band] += jnp.where(first == band, term, 0.0)
        for side in range(2):
            plane = pair * 2 + side
            for band in range(bands):
                out_ref[band, plane] = totals[side][band].astype(out_ref.dtype)
                for other in range(bands):
                    product = own_ref[other, plane].astype(F32) * totals[side][band]
                    sums[other * bands + band] += product.reshape(length // 8, 8, length).sum(axis=0)
        if pair:
            for copy in copies(pair - 1):
                copy.start()

    for entry in range(bands * bands):
        row = jnp.sum(sums[entry], axis=0, keepdims=True)
        terms_ref[:, entry // bands, entry % bands : entry % bands + 1, :] = jnp.broadcast_to(
            row[None], (terms_ref.shape[0], 1, row.shape[1])
        )
    for copy in copies(planes // 2 - 1):
        copy.start()
    for pair in range(planes // 2):
        for copy in copies(pair):
            copy.wait()


VMEM = pl.BlockSpec(memory_space=pltpu.VMEM)
SMEM = pl.BlockSpec(memory_space=pltpu.SMEM)
ANY = pl.BlockSpec(memory_space=pl.ANY)


def on_device(right, left, own_orbitals, resident_orbitals, pair_lists, pair_counts):
    bands, planes, length = own_orbitals.shape[:3]
    pieces = lax.axis_size("grid")
    rows = length // pieces
    received = passed_along(resident_orbitals, "band", 1)
    lists, counts = pair_lists, pair_counts
    field = pltpu.VMEM((planes, length, length), F32)

    table = pltpu.VMEM((4, length, length), F32)

    def coded(slots, share):
        tiles = slots * planes + (-(-slots // share) if share else 0)
        return jax.ShapeDtypeStruct((pieces, tiles, rows, length), jnp.int16)

    early, kernel, codes, index = pl.pallas_call(
        early_kernel,
        out_shape=(
            coded(2, 0),
            jax.ShapeDtypeStruct((length, rows * length), F32),
            jax.ShapeDtypeStruct((2, length, length), F32),
            jax.ShapeDtypeStruct((1,), jnp.int32),
        ),
        in_specs=[SMEM, SMEM, ANY, ANY, VMEM, VMEM],
        out_specs=(VMEM, VMEM, VMEM, SMEM),
        scratch_shapes=[
            field,
            pltpu.VMEM(own_orbitals.shape, BF16),
            pltpu.VMEM(own_orbitals.shape, BF16),
            pltpu.SemaphoreType.DMA((2,)),
        ],
        cost_estimate=pl.CostEstimate(
            flops=600_000_000, bytes_accessed=3_000_000, transcendentals=0
        ),
        compiler_params=LIMIT,
        name="early",
    )(lists, counts, own_orbitals, resident_orbitals, right, left)

    def branch(slots):
        def run(own_orbitals, resident_orbitals, received, lists, counts, early, kernel, codes, right, left):
            sent = pl.pallas_call(
                functools.partial(late_kernel, slots),
                out_shape=coded(slots, OUT_SHARE),
                in_specs=[SMEM, SMEM, VMEM, VMEM, VMEM, VMEM, VMEM, VMEM],
                out_specs=VMEM,
                scratch_shapes=[pltpu.VMEM((2, planes, length, length), F32), table],
                compiler_params=LIMIT,
                name="late",
            )(lists, counts, own_orbitals, received, early, codes, right, left)
            got = lax.all_to_all(sent, "grid", split_axis=0, concat_axis=0, tiled=True)
            sent = pl.pallas_call(
                functools.partial(middle_kernel, slots, planes),
                out_shape=coded(slots, BACK_SHARE),
                in_specs=[VMEM, VMEM, VMEM],
                out_specs=VMEM,
                scratch_shapes=[pltpu.VMEM((slots, length * rows, length), F32)] * 2 + [table],
                compiler_params=LIMIT,
                name="middle",
            )(got, kernel, left)
            got = lax.all_to_all(sent, "grid", split_axis=0, concat_axis=0, tiled=True)
            return pl.pallas_call(
                functools.partial(final_kernel, slots),
                out_shape=(
                    jax.ShapeDtypeStruct(own_orbitals.shape, BF16),
                    jax.ShapeDtypeStruct((pieces, bands, bands, length), F32),
                ),
                in_specs=[SMEM, SMEM, VMEM, VMEM, VMEM, VMEM, VMEM, VMEM],
                out_specs=(ANY, VMEM),
                scratch_shapes=[
                    pltpu.VMEM((slots, length, length), F32),
                    pltpu.VMEM((bands * bands, 8, length), F32),
                    pltpu.VMEM(own_orbitals.shape, BF16),
                    pltpu.SemaphoreType.DMA((planes // 2, bands)),
                ],
                compiler_params=LIMIT,
                name="final",
            )(lists, counts, own_orbitals, resident_orbitals, received, got, right, left)

        return run

    exchange, terms = lax.switch(
        index[0],
        [branch(2), branch(3), branch(4)],
        own_orbitals,
        resident_orbitals,
        received,
        lists,
        counts,
        early,
        kernel,
        codes,
        right,
        left,
    )
    terms = lax.all_to_all(terms, "grid", split_axis=0, concat_axis=0, tiled=True)
    return exchange, jnp.sum(terms, axis=(0, 3))


def solution(mesh):
    in_specs = (
        P(None, None),
        P(None, None),
        P("band", "grid", None, None),
        P("band", "grid", None, None),
        P("band", None, None, None),
        P("band", None),
    )
    out_specs = (P("band", "grid", None, None), P("band", None))
    mapped = jax.shard_map(
        on_device, mesh=mesh, in_specs=in_specs, out_specs=out_specs, check_vma=False
    )

    def step(own_orbitals, resident_orbitals, pair_lists, pair_counts):
        length = own_orbitals.shape[-1]
        right, left = jnp.asarray(right_table(length)), jnp.asarray(left_table(length))
        return mapped(right, left, own_orbitals, resident_orbitals, pair_lists, pair_counts)

    return step
```
